512 devices in a mesh: grp: 4 (over z_hi, core), row: 4 (over x), col: 32 (over y, z_lo).
Axes of the slice: x: 4, y: 4, z: 16 (z_hi: 2, z_lo: 8; z = z_hi * 8 + z_lo), core: 2. Of those that a mesh axis runs over, the one named last changes fastest.
Arguments:
- acts: bfloat16 [768, 8192], P('grp', 'col'), may hold values from -6 to 6
- grads: bfloat16 [768, 28672], P('grp', ('row', 'col')), may hold values from -6 to 6
- basis_in: bfloat16 [8192, 4096], P('col', 'row'), may hold values from -0.0625 to 0.0625
- basis_out: bfloat16 [4, 7168, 14336], P('row', 'grp', 'col'), may hold values from -0.03125 to 0.03125
- lengths: int32 [4, 2], P('grp'), may hold values from 1 to 96, 144 in all within a row
Outputs:
- eigenvalues: float32 [14336, 4096], P('col', 'row')
The draws below stay inside these ranges and needn't reach their ends.
Inputs may be any that keep to these rules, and one draw needn't show every extreme that they name: The 2 lengths of each index of grp sum to exactly 144, and none exceeds 96.
All inputs are finite; a program needn't handle non-finite values.
Results may differ from the reference program's by a relative error of at most 0.006.
Values may be sent and summed in bfloat16 or wider, within the bound.
No kernel may reach another device: no remote copies, remote signals or barrier semaphores. Data moves between devices by JAX's collectives and lax.ppermute only.
A program may use at most 64 MiB of HBM per device.

```python
import math
import jax
import jax.numpy as jnp
import numpy as np
from jax import lax

FI = 8192
FO = 28672
IW = 4096
GW = 14336
LEN = 96
SEQS = 2
VALID = 144
TOKENS = 768
N_GRP = 4
N_ROW = 4


def levels(stream_key, dims, shards, least, largest):
    factor_of = 1.0
    for position, blocks in shards:
        steps = jax.random.uniform(jax.random.fold_in(jax.random.fold_in(stream_key, 6), position), (blocks,), jnp.float32, least / len(shards), largest / len(shards))
        factor_of = factor_of * jnp.repeat(jnp.exp(steps), dims[position] // blocks).reshape((-1,) + (1,) * (len(dims) - 1 - position))
    return factor_of


def profile(count, total, reach, skew):
    loads = [(1 << 20) // math.isqrt(standing ** skew) + 1 for standing in range(2, count + 1)]
    rest, counts = total - reach - (count - 1), [1] * (count - 1)
    while rest > 0:
        candidates = [i for i in range(count - 1) if counts[i] < reach]
        mass, remaining = sum([loads[i] for i in candidates]), rest
        for i in candidates:
            extra = min(reach - counts[i], max(1, remaining * loads[i] // mass), rest)
            counts[i] = counts[i] + extra
            rest = rest - extra
    return np.array([reach] + counts)


def ragged(own_key, count, total, reach, lean):
    if count == 2:
        one = jax.random.randint(own_key, (), max(1, total - reach), min(reach, total - 1) + 1)
        return jnp.stack([one, total - one])
    sizes = jnp.asarray(profile(count, total, reach, lean), jnp.int32)
    couples = (count - 1) // 2
    source_of, sink = sizes[1:1 + 2 * couples:2], sizes[2:2 + 2 * couples:2]
    slack = jnp.minimum(source_of - 1, reach - sink)
    shifted = jax.random.randint(jax.random.fold_in(own_key, 1), (couples,), 0, 1 << 20) % (slack + 1)
    sizes = sizes.at[1:1 + 2 * couples:2].set(source_of - shifted).at[2:2 + 2 * couples:2].set(sink + shifted)
    return sizes[jax.random.permutation(jax.random.fold_in(own_key, 2), count)]


def bell_draw(key, dims, spread, most, shards=(), kind=jnp.bfloat16):
    entries = jax.random.normal(key, dims, jnp.float32) * spread
    if len(shards) > 0:
        entries = levels(key, dims, shards, -0.22, 0.18) * entries
    return jnp.clip(entries, min=-most, max=most).astype(kind)


def setup_inputs(seed: int = 0) -> dict:
    key_list = jax.random.split(jax.random.key(seed), 6)
    return {
        "acts": bell_draw(key_list[0], (TOKENS, FI), 1.0, 6.0, ((0, 4), (1, 32))),
        "grads": bell_draw(key_list[1], (TOKENS, FO), 1.0, 6.0, ((0, 4), (1, 128))),
        "basis_in": bell_draw(key_list[2], (FI, IW), FI ** -0.5, 0.0625, ((0, 32), (1, 4))),
        "basis_out": bell_draw(key_list[3], (N_ROW, FO // N_ROW, GW), FO ** -0.5, 0.03125, ((0, 4), (1, 4), (2, 32))),
        "lengths": jax.vmap(lambda own: ragged(own, SEQS, VALID, LEN, 2))(jax.random.split(key_list[4], N_GRP)).reshape((N_GRP, SEQS)).astype(jnp.int32),
    }


def reference(acts, grads, basis_in, basis_out, lengths):
    proj_in = jnp.dot(acts, basis_in, preferred_element_type=jnp.float32).astype(jnp.bfloat16)
    whole_basis = basis_out.reshape(FO, GW)
    proj_out = jnp.dot(grads, whole_basis, preferred_element_type=jnp.float32).astype(jnp.bfloat16)
    count = N_GRP * SEQS
    slots = jnp.arange(LEN).astype(jnp.int32)
    valid = (slots[None, None, :] < lengths[:, :, None]).reshape(count, LEN).astype(proj_out.dtype)

    def step(total, item):
        grad_seq, act_seq, keep = item
        chosen = grad_seq * keep[:, None]
        block = jnp.dot(chosen.T, act_seq, preferred_element_type=jnp.float32)
        return total + block * block, None

    total, unused = lax.scan(step, jnp.zeros((GW, IW), jnp.float32),
                             (proj_out.reshape(count, LEN, GW), proj_in.reshape(count, LEN, IW), valid))
    return total / (count * LEN)
```

```python
import jax
import jax.numpy as jnp
from jax import lax
from jax.experimental import pallas as pl
from jax.experimental.pallas import tpu as pltpu
from jax.sharding import Mesh, PartitionSpec as P

LEN = 96
VALID = 144
BF = jnp.bfloat16
F32 = jnp.float32
PLANE = ("zhi", "core", "y", "zlo")


def transposed():
    def place(zhi, core, y, zlo):
        return ((zhi * 2 + core) * 4 + y) * 8 + zlo

    pairs = []
    for g in range(4):
        for y in range(4):
            for z in range(8):
                to = 7 - z if g >> 1 != y >> 1 else z
                pairs.append((place(g >> 1, g & 1, y, z), place(y >> 1, y & 1, g, to)))
    return pairs


def exchange(x, axis):
    return lax.all_to_all(x, axis, 0, 0, tiled=True)


def everywhere(x, axis):
    n = lax.axis_size(axis)
    return lax.all_to_all(jnp.broadcast_to(x[None], (n,) + x.shape), axis, 0, 0, tiled=True)


def swap(x, axis, by):
    n = lax.axis_size(axis)
    return lax.ppermute(x, axis, [(i, i ^ by) for i in range(n)])


def project_kernel(lines_ref, basis_ref, out_ref):
    for t in range(4):
        total = jnp.zeros((VALID, basis_ref.shape[1]), F32)
        for z in range(8):
            total += jnp.dot(
                lines_ref[t, z, :, :224],
                basis_ref[z * 224 : (z + 1) * 224, :],
                preferred_element_type=F32,
            )
        out_ref[t] = total.astype(BF)


def square_kernel(out_ref, in_ref, mask_ref, eig_ref):
    total = jnp.zeros(eig_ref.shape, F32)
    for g in range(4):
        first = out_ref[g] * mask_ref[g]
        for left in (first, out_ref[g] - first):
            block = lax.dot_general(
                left, in_ref[g], (((0,), (0,)), ((), ())), preferred_element_type=F32
            )
            total += block * block
    eig_ref[...] = total / 768.0


def project(lines, basis):
    return pl.pallas_call(
        project_kernel,
        out_shape=jax.ShapeDtypeStruct((4, VALID, basis.shape[1]), BF),
        compiler_params=pltpu.CompilerParams(vmem_limit_bytes=40 << 20),
    )(lines, basis)


def squares(proj_out, proj_in, mask):
    cols, wide = proj_out.shape[2], proj_in.shape[2]
    tile = 256
    return pl.pallas_call(
        square_kernel,
        grid=(wide // tile,),
        in_specs=[
            pl.BlockSpec((4, VALID, cols), lambda i: (0, 0, 0)),
            pl.BlockSpec((4, VALID, tile), lambda i: (0, 0, i)),
            pl.BlockSpec((4, VALID, 1), lambda i: (0, 0, 0)),
        ],
        out_specs=pl.BlockSpec((cols, tile), lambda i: (0, i)),
        out_shape=jax.ShapeDtypeStruct((cols, wide), F32),
        compiler_params=pltpu.CompilerParams(vmem_limit_bytes=40 << 20),
    )(proj_out, proj_in, mask)


def per_device(acts, grads, basis_in, basis_out, lengths):
    first = lengths[0, 0]
    slot = jnp.arange(VALID, dtype=jnp.int32)
    source = jnp.where(slot < first, slot, slot - first + LEN)
    mask = (slot < first).astype(BF)
    lines = jnp.take(grads, source, axis=0)
    lines = jnp.concatenate([lines, jnp.broadcast_to(mask[:, None], (VALID, 32))], axis=1)
    lines = lax.ppermute(lines, PLANE, transposed())
    partial = jnp.dot(jnp.take(acts, source, axis=0), basis_in, preferred_element_type=F32)
    partial = partial.astype(BF).reshape(VALID, 8, 4, 32).transpose(2, 0, 1, 3)
    partial = exchange(partial.reshape(4, VALID, 256), "y")
    partial = jnp.sum(partial.astype(F32), axis=0).astype(BF)
    both = jnp.concatenate(
        [
            jnp.broadcast_to(lines[None, :, :224], (8, VALID, 224)),
            partial.reshape(VALID, 8, 32).transpose(1, 0, 2),
        ],
        axis=2,
    )
    both = exchange(both, "zlo")
    proj_in = jnp.sum(both[:, :, 224:].astype(F32), axis=0).astype(BF)
    mirrored = (lax.axis_index("zhi") != lax.axis_index("y") // 2)
    feats = both[:, :, :224]
    feats = jnp.where(mirrored, feats[::-1], feats)
    spare = jnp.concatenate(
        [proj_in[None], jnp.broadcast_to(lines[None, :, 224:], (7, VALID, 32))], axis=0
    )
    whole = everywhere(jnp.concatenate([feats, spare], axis=2), "y")
    part = project(whole, basis_out[0])
    masks = whole[:, 1, :, 224:225]
    proj_in = whole[:, 0, :, 224:].transpose(1, 0, 2).reshape(VALID, 128)
    ins = jnp.stack([proj_in, swap(proj_in, "zhi", 1)])
    ins = jnp.where(lax.axis_index("zhi") == 0, ins, ins[::-1])
    zlo = lax.axis_index("zlo")
    for by in (4, 2, 1):
        other = swap(ins, "zlo", by)
        low = (zlo // by) % 2 == 0
        ins = jnp.where(
            low, jnp.concatenate([ins, other], axis=2), jnp.concatenate([other, ins], axis=2)
        )
    wide = ins.shape[2]
    ins = ins.reshape(2, VALID, 2, 2, 2, 128).transpose(0, 1, 4, 3, 2, 5).reshape(2, VALID, wide)
    other = swap(ins, "core", 1)
    core0 = lax.axis_index("core") == 0
    ins = jnp.where(core0, jnp.stack([ins, other], axis=1), jnp.stack([other, ins], axis=1))
    ins = ins.reshape(4, VALID, wide)
    cols = part.shape[2]
    half = exchange(part.reshape(2, 2 * VALID, cols), "core").astype(F32).sum(0).astype(BF)
    own = exchange(half.reshape(4, VALID // 2, cols), "x").astype(F32).sum(0).astype(BF)
    own = (own.astype(F32) + swap(own, "zhi", 1).astype(F32)).astype(BF)
    half = everywhere(own, "x").reshape(2 * VALID, cols)
    outs = everywhere(half, "core").reshape(4, VALID, cols)
    return squares(outs, ins, masks)


def solution(mesh):
    fine = Mesh(mesh.devices.reshape(2, 2, 4, 4, 8), ("zhi", "core", "x", "y", "zlo"))
    grp, row, col = ("zhi", "core"), "x", ("y", "zlo")
    in_specs = (
        P(grp, col),
        P(grp, (row, *col)),
        P(col, row),
        P(row, grp, col),
        P(grp, None),
    )
    return jax.shard_map(
        per_device, mesh=fine, in_specs=in_specs, out_specs=P(col, row), check_vma=False
    )
```

```python
import jax
import jax.numpy as jnp
from jax import lax
from jax.experimental import pallas as pl
from jax.experimental.pallas import tpu as pltpu
from jax.sharding import Mesh, PartitionSpec as P

LEN = 96
VALID = 144
FEAT = 224
WIDE = 256
BF = jnp.bfloat16
F32 = jnp.float32
PLANE = ("zhi", "core", "y", "zh", "zq")
PARAMS = pltpu.CompilerParams(vmem_limit_bytes=48 << 20)


def to_basis(flip):
    def place(zhi, core, y, zlo):
        return ((zhi * 2 + core) * 4 + y) * 8 + zlo

    pairs = []
    for zhi in range(2):
        for core in range(2):
            for y in range(4):
                for z in range(8):
                    to = 7 - z if zhi != y >> 1 else z
                    there = place(y >> 1, zhi, core * 2 + (y & 1), to ^ flip)
                    pairs.append((place(zhi, core, y, z), there))
    return pairs


def exchange(x, axis):
    return lax.all_to_all(x, axis, 0, 0, tiled=True)


def everywhere(x, axis):
    return exchange(jnp.broadcast_to(x[None], (lax.axis_size(axis),) + x.shape), axis)


def swap(x, axis):
    return lax.ppermute(x, axis, [(0, 1), (1, 0)])


def across(left, right):
    return lax.dot_general(left, right, (((1,), (1,)), ((), ())), preferred_element_type=F32)


def chosen(first):
    slot = lax.broadcasted_iota(jnp.int32, (VALID, 2 * LEN), 0)
    line = lax.broadcasted_iota(jnp.int32, (VALID, 2 * LEN), 1)
    source = jnp.where(slot < first, slot, slot - first + LEN)
    return (source == line).astype(F32).astype(BF)


def start_kernel(len_ref, grads_ref, acts_ref, basis_ref, lines_ref, part_ref):
    pick = chosen(len_ref[0, 0])
    lines_ref[:, :FEAT] = jnp.dot(pick, grads_ref[...], preferred_element_type=F32).astype(BF)
    lines_ref[:, FEAT:] = jnp.zeros((VALID, WIDE - FEAT), BF)
    lines = jnp.dot(pick, acts_ref[...], preferred_element_type=F32).astype(BF)
    for y in range(4):
        part_ref[y] = jnp.dot(
            lines, basis_ref[:, y * WIDE : (y + 1) * WIDE], preferred_element_type=F32
        ).astype(BF)


def join_kernel(near_ref, far_ref, parts_ref, out_ref):
    total = parts_ref[0].astype(F32)
    for y in range(1, 4):
        total += parts_ref[y].astype(F32)
    total = total.astype(BF)
    for d in range(4):
        for w, ref in enumerate((near_ref, far_ref)):
            at = d * 64 + w * 32
            out_ref[d, w] = jnp.concatenate([ref[:, :FEAT], total[:, at : at + 32]], axis=1)


def sort_kernel(where_ref, both_ref, out_ref, in_ref):
    zh, mirrored = where_ref[0], where_ref[1]
    for f in range(8):
        at = jnp.where(mirrored == 1, 7 - f, f)
        far = (at // 4 != zh).astype(jnp.int32)
        block = both_ref[at % 4, far][:, :FEAT]
        for copy in range(4):
            out_ref[copy, :, f * FEAT : (f + 1) * FEAT] = block
    sums = []
    for w in range(2):
        total = both_ref[0, w][:, FEAT:].astype(F32)
        for q in range(1, 4):
            total += both_ref[q, w][:, FEAT:].astype(F32)
        sums.append(total)
    slot = lax.broadcasted_iota(jnp.int32, (VALID, 64), 0)
    mask = (slot < where_ref[2]).astype(F32)
    in_ref[...] = jnp.concatenate(sums + [mask], axis=1).astype(BF)


def project_kernel(where_ref, lines_ref, own_ref, other_ref, out_ref):
    core = where_ref[3]
    for t in range(2):
        total = across(lines_ref[2 * t + core], own_ref[...])
        total += across(lines_ref[2 * t + 1 - core], other_ref[...])
        for h in range(2):
            out_ref[2 * t + h] = total[h * 72 : (h + 1) * 72].astype(BF)


def sum_kernel(parts_ref, out_ref):
    total = parts_ref[0].astype(F32)
    for x in range(1, 4):
        total += parts_ref[x].astype(F32)
    out_ref[...] = total.astype(BF)


def spread_kernel(one_ref, two_ref, out_ref):
    total = (one_ref[...].astype(F32) + two_ref[...].astype(F32)).astype(BF)
    for x in range(4):
        out_ref[x] = total


def arrange_kernel(where_ref, own_ref, other_ref, own_mask_ref, other_mask_ref, out_ref, mask_ref):
    core, zq = where_ref[3], where_ref[4]
    for zhi in range(2):
        for c in range(2):
            mine = core == c
            g = zhi * 2 + c
            for y in range(4):
                for q in range(4):
                    at = y * WIDE + q * 64
                    block = jnp.where(mine, own_ref[y, q ^ zq], other_ref[y, q ^ zq])
                    out_ref[g, :, at : at + 64] = block[:, zhi * 64 : zhi * 64 + 64]
            mask_ref[g] = jnp.where(mine, own_mask_ref[zhi], other_mask_ref[zhi])


def square_kernel(where_ref, own_ref, other_ref, in_ref, mask_ref, eig_ref, left_ref):
    core = where_ref[3]
    for g in range(4):
        mine = core == g // 2
        lines = jnp.where(mine, own_ref[g % 2], other_ref[g % 2])
        first = lines * mask_ref[g][:, :1]
        left_ref[2 * g] = first.T
        left_ref[2 * g + 1] = (lines - first).T
    rows, cols = 112, 256
    for o in range(448 // rows):
        for i in range(1024 // cols):
            total = jnp.zeros((rows, cols), F32)
            for s in range(8):
                block = jnp.dot(
                    left_ref[s, o * rows : (o + 1) * rows, :],
                    in_ref[s // 2, :, i * cols : (i + 1) * cols],
                    preferred_element_type=F32,
                )
                total += block * block
            eig_ref[o * rows : (o + 1) * rows, i * cols : (i + 1) * cols] = total / 768.0


def call(kernel, out, *args, scalars=1, scratch=()):
    single = not isinstance(out, (list, tuple))
    smem = pl.BlockSpec(memory_space=pltpu.SMEM)
    vmem = pl.BlockSpec(memory_space=pltpu.VMEM)
    outs = [out] if single else list(out)
    got = pl.pallas_call(
        kernel,
        in_specs=[smem] * scalars + [vmem] * (len(args) - scalars),
        out_specs=[vmem] * len(outs),
        out_shape=outs,
        scratch_shapes=scratch,
        compiler_params=PARAMS,
    )(*args)
    return got[0] if single else got


def like(*shape, dtype=BF):
    return jax.ShapeDtypeStruct(shape, dtype)


def per_device(acts, grads, basis_in, basis_out, lengths):
    zhi, core, zh, zq = (lax.axis_index(a) for a in ("zhi", "core", "zh", "zq"))
    where = jnp.stack([zh, (core != zhi).astype(jnp.int32), lengths[0, 0], core, zq])
    lines, partial = call(
        start_kernel,
        [like(VALID, WIDE), like(4, VALID, WIDE)],
        lengths,
        grads,
        acts,
        basis_in,
    )
    near = lax.ppermute(lines, PLANE, to_basis(0))
    far = lax.ppermute(lines, PLANE, to_basis(4))
    basis = basis_out[0].T
    other_basis = swap(basis, "core")
    partial = exchange(partial, "y")
    both = call(join_kernel, like(4, 2, VALID, WIDE), near, far, partial, scalars=0)
    both = exchange(both, "zq")
    lines, ins = call(sort_kernel, [like(4, VALID, 8 * FEAT), like(VALID, 128)], where, both)
    lines = exchange(lines, "y")
    sums = ins.astype(F32) + swap(ins, "zh").astype(F32)
    ins = jnp.concatenate([sums[:, :64].astype(BF), ins[:, 64:]], axis=1)
    pair = swap(ins, "zhi")
    low = zhi == 0
    pair = jnp.where(low, jnp.stack([ins, pair]), jnp.stack([pair, ins]))
    masks = pair[:, :, 64:]
    ins = jnp.concatenate([pair[0, :, :64], pair[1, :, :64]], axis=1)
    ins, masks, other_masks, lines = lax.optimization_barrier(
        (ins, masks, swap(masks, "core"), lines)
    )
    ins = jnp.stack([ins] + [lax.ppermute(ins, "zq", [(i, i ^ k) for i in range(4)]) for k in (1, 2, 3)])
    cols = basis.shape[0]
    part = call(project_kernel, like(4, 72, cols), where, lines, basis, other_basis)
    part = exchange(part, "x")
    part = call(sum_kernel, like(72, cols), part, scalars=0)
    part, ins = lax.optimization_barrier((part, ins))
    ins = everywhere(ins, "y").reshape(4, 4, VALID, 128)
    part = call(spread_kernel, like(4, 72, cols), part, swap(part, "zhi"), scalars=0)
    part, ins = lax.optimization_barrier((part, ins))
    outs = exchange(part, "x").reshape(2, VALID, cols)
    ins, masks = call(
        arrange_kernel,
        [like(4, VALID, 1024), like(4, VALID, 64)],
        where,
        ins,
        swap(ins, "core"),
        masks,
        other_masks,
    )
    return call(
        square_kernel,
        like(cols, 1024, dtype=F32),
        where,
        outs,
        swap(outs, "core"),
        ins,
        masks,
        scratch=[pltpu.VMEM((8, cols, VALID), BF)],
    )


def solution(mesh):
    axes = ("zhi", "core", "x", "y", "zh", "zq")
    fine = Mesh(mesh.devices.reshape(2, 2, 4, 4, 2, 4), axes)
    grp, row, col = ("zhi", "core"), "x", ("y", "zh", "zq")
    in_specs = (
        P(grp, col),
        P(grp, (row, *col)),
        P(col, row),
        P(row, grp, col),
        P(grp, None),
    )
    return jax.shard_map(
        per_device, mesh=fine, in_specs=in_specs, out_specs=P(col, row), check_vma=False
    )
```

```python
import jax
import jax.numpy as jnp
from jax import lax
from jax.experimental import pallas as pl
from jax.experimental.pallas import tpu as pltpu
from jax.sharding import Mesh, PartitionSpec as P

LEN = 96
VALID = 144
FEAT = 224
WIDE = 256
BF = jnp.bfloat16
F32 = jnp.float32
PLANE = ("zhi", "core", "y", "zh", "zq")
PARAMS = pltpu.CompilerParams(vmem_limit_bytes=48 << 20)


def to_basis(flip):
    def place(zhi, core, y, zlo):
        return ((zhi * 2 + core) * 4 + y) * 8 + zlo

    pairs = []
    for zhi in range(2):
        for core in range(2):
            for y in range(4):
                for z in range(8):
                    to = 7 - z if zhi != y >> 1 else z
                    there = place(y >> 1, zhi, core * 2 + (y & 1), to ^ flip)
                    pairs.append((place(zhi, core, y, z), there))
    return pairs


def exchange(x, axis):
    return lax.all_to_all(x, axis, 0, 0, tiled=True)


def everywhere(x, axis):
    return exchange(jnp.broadcast_to(x[None], (lax.axis_size(axis),) + x.shape), axis)


def swap(x, axis):
    return lax.ppermute(x, axis, [(0, 1), (1, 0)])


def across(left, right):
    return lax.dot_general(left, right, (((1,), (1,)), ((), ())), preferred_element_type=F32)


def chosen(first):
    slot = lax.broadcasted_iota(jnp.int32, (VALID, 2 * LEN), 0)
    line = lax.broadcasted_iota(jnp.int32, (VALID, 2 * LEN), 1)
    source = jnp.where(slot < first, slot, slot - first + LEN)
    return (source == line).astype(F32).astype(BF)


def pack_kernel(len_ref, grads_ref, out_ref):
    pick = chosen(len_ref[0, 0])
    out_ref[:, :FEAT] = jnp.dot(pick, grads_ref[...], preferred_element_type=F32).astype(BF)
    out_ref[:, FEAT:] = jnp.zeros((VALID, WIDE - FEAT), BF)


def inputs_kernel(where_ref, acts_ref, basis_ref, *out_refs):
    pick = chosen(where_ref[2])
    lines = jnp.dot(pick, acts_ref[...], preferred_element_type=F32).astype(BF)
    for k in range(4):
        at = pl.multiple_of((where_ref[5] ^ k) * WIDE, WIDE)
        out_refs[k][...] = jnp.dot(
            lines, basis_ref[:, pl.ds(at, WIDE)], preferred_element_type=F32
        ).astype(BF)


def join_kernel(near_ref, far_ref, *refs):
    parts, out_ref = refs[:4], refs[4]
    total = parts[0][...].astype(F32)
    for k in range(1, 4):
        total += parts[k][...].astype(F32)
    total = total.astype(BF)
    for d in range(4):
        for w, ref in enumerate((near_ref, far_ref)):
            at = d * 64 + w * 32
            out_ref[d, w] = jnp.concatenate([ref[:, :FEAT], total[:, at : at + 32]], axis=1)


def sort_kernel(where_ref, both_ref, out_ref, in_ref):
    zh, mirrored = where_ref[0], where_ref[1]
    for f in range(8):
        at = jnp.where(mirrored == 1, 7 - f, f)
        far = (at // 4 != zh).astype(jnp.int32)
        out_ref[:, f * FEAT : (f + 1) * FEAT] = both_ref[at % 4, far][:, :FEAT]
    sums = []
    for w in range(2):
        total = both_ref[0, w][:, FEAT:].astype(F32)
        for q in range(1, 4):
            total += both_ref[q, w][:, FEAT:].astype(F32)
        sums.append(total)
    half = VALID // 2
    packed = jnp.concatenate([x[i : i + half] for i in (0, half) for x in sums], axis=1)
    count = jnp.full((8, 128), where_ref[2], jnp.int32).astype(F32).astype(BF)
    for copy in range(16):
        in_ref[copy, :half] = packed.astype(BF)
        in_ref[copy, half:] = count


def merge_kernel(parts_ref, out_ref):
    half = VALID // 2
    for zhi in range(2):
        for q in range(4):
            at = zhi * 8 + q
            total = parts_ref[at, :half].astype(F32) + parts_ref[at + 4, :half].astype(F32)
            total = total.astype(BF)
            out_ref[zhi, :half, q * 64 : q * 64 + 64] = total[:, :64]
            out_ref[zhi, half:VALID, q * 64 : q * 64 + 64] = total[:, 64:]
        for h in range(2):
            out_ref[zhi, VALID:, h * 128 : h * 128 + 128] = parts_ref[zhi * 8, half:]


def order_kernel(where_ref, own_ref, other_ref, one_ref, two_ref):
    same = where_ref[3] == where_ref[6]
    own, other = own_ref[...], other_ref[...]
    one_ref[...] = jnp.where(same, own, other).T
    two_ref[...] = jnp.where(same, other, own).T


def project_kernel(where_ref, a_ref, b_ref, c_ref, d_ref, one_ref, two_ref, out_ref):
    yh = where_ref[7]
    for left, right, t in ((a_ref, b_ref, yh), (c_ref, d_ref, 1 - yh)):
        total = jnp.dot(left[...], one_ref[...], preferred_element_type=F32)
        total += jnp.dot(right[...], two_ref[...], preferred_element_type=F32)
        for h in range(2):
            out_ref[2 * t + h] = total[h * 72 : (h + 1) * 72].astype(BF)


def sum_kernel(parts_ref, out_ref):
    total = parts_ref[0].astype(F32)
    for x in range(1, 4):
        total += parts_ref[x].astype(F32)
    out_ref[...] = total.astype(BF)


def spread_kernel(one_ref, two_ref, out_ref):
    total = (one_ref[...].astype(F32) + two_ref[...].astype(F32)).astype(BF)
    for x in range(4):
        out_ref[x] = total


def arrange_kernel(where_ref, own_ref, other_ref, out_ref, mask_ref):
    core = where_ref[3]
    slot = lax.broadcasted_iota(jnp.int32, (VALID, 128), 0).astype(F32)
    for zhi in range(2):
        for c in range(2):
            mine = core == c
            g = zhi * 2 + c
            for y in range(4):
                k = y ^ where_ref[5]
                block = jnp.where(mine, own_ref[k, zhi], other_ref[k, zhi])
                out_ref[g, :, y * WIDE : (y + 1) * WIDE] = block[:VALID]
            count = block[VALID : VALID + 1, :128].astype(F32)
            mask_ref[g] = (slot < count).astype(F32).astype(BF)


def square_kernel(where_ref, own_ref, other_ref, in_ref, mask_ref, eig_ref, left_ref):
    core = where_ref[3]
    for g in range(4):
        mine = core == g // 2
        lines = jnp.where(mine, own_ref[g % 2], other_ref[g % 2])
        first = lines * mask_ref[g][:, :1]
        left_ref[2 * g] = first.T
        left_ref[2 * g + 1] = (lines - first).T
    rows, cols = 112, 256
    for o in range(448 // rows):
        for i in range(1024 // cols):
            total = jnp.zeros((rows, cols), F32)
            for s in range(8):
                block = jnp.dot(
                    left_ref[s, o * rows : (o + 1) * rows, :],
                    in_ref[s // 2, :, i * cols : (i + 1) * cols],
                    preferred_element_type=F32,
                )
                total += block * block
            eig_ref[o * rows : (o + 1) * rows, i * cols : (i + 1) * cols] = total / 768.0


def call(kernel, out, *args, scalars=1, scratch=()):
    single = not isinstance(out, (list, tuple))
    smem = pl.BlockSpec(memory_space=pltpu.SMEM)
    vmem = pl.BlockSpec(memory_space=pltpu.VMEM)
    outs = [out] if single else list(out)
    got = pl.pallas_call(
        kernel,
        in_specs=[smem] * scalars + [vmem] * (len(args) - scalars),
        out_specs=[vmem] * len(outs),
        out_shape=outs,
        scratch_shapes=scratch,
        compiler_params=PARAMS,
    )(*args)
    return got[0] if single else got


def like(*shape, dtype=BF):
    return jax.ShapeDtypeStruct(shape, dtype)


def others(x, axis):
    n = lax.axis_size(axis)
    return [lax.ppermute(x, axis, [(i, i ^ k) for i in range(n)]) for k in range(1, n)]


def per_device(acts, grads, basis_in, basis_out, lengths):
    zhi, core, y, zh, zq = (lax.axis_index(a) for a in ("zhi", "core", "y", "zh", "zq"))
    crossed = (core != zhi).astype(jnp.int32)
    where = jnp.stack([zh, crossed, lengths[0, 0], core, zq, y, y & 1, y >> 1])
    lines = call(pack_kernel, like(VALID, WIDE), lengths, grads)
    near = lax.ppermute(lines, PLANE, to_basis(0))
    far = lax.ppermute(lines, PLANE, to_basis(4))
    partial = call(inputs_kernel, [like(VALID, WIDE)] * 4, where, acts, basis_in)
    partial = [partial[0]] + [
        lax.ppermute(partial[k], "y", [(i, i ^ k) for i in range(4)]) for k in (1, 2, 3)
    ]
    basis = basis_out[0].T
    cols, rows = basis.shape
    other_basis = swap(basis, "core")
    both = call(join_kernel, like(4, 2, VALID, WIDE), near, far, *partial, scalars=0)
    both = exchange(both, "zq")
    lines, ins = call(sort_kernel, [like(VALID, 8 * FEAT), like(16, 80, 128)], where, both)
    one, two = call(order_kernel, [like(rows, cols)] * 2, where, basis, other_basis)
    lines = [lines] + others(lines, "y")
    ins = exchange(ins, ("zhi", "zh", "zq"))
    ins = call(merge_kernel, like(2, VALID + 8, WIDE), ins, scalars=0)
    ins, lines, one, two = lax.optimization_barrier((ins, lines, one, two))
    part = call(project_kernel, like(4, 72, cols), where, *lines, one, two)
    part = exchange(part, "x")
    part = call(sum_kernel, like(72, cols), part, scalars=0)
    part, ins = lax.optimization_barrier((part, ins))
    ins = jnp.stack([ins] + others(ins, "y"))
    part = call(spread_kernel, like(4, 72, cols), part, swap(part, "zhi"), scalars=0)
    part, ins = lax.optimization_barrier((part, ins))
    outs = exchange(part, "x").reshape(2, VALID, cols)
    ins, masks = call(
        arrange_kernel,
        [like(4, VALID, 1024), like(4, VALID, 128)],
        where,
        ins,
        swap(ins, "core"),
    )
    return call(
        square_kernel,
        like(cols, 1024, dtype=F32),
        where,
        outs,
        swap(outs, "core"),
        ins,
        masks,
        scratch=[pltpu.VMEM((8, cols, VALID), BF)],
    )


def solution(mesh):
    axes = ("zhi", "core", "x", "y", "zh", "zq")
    fine = Mesh(mesh.devices.reshape(2, 2, 4, 4, 2, 4), axes)
    grp, row, col = ("zhi", "core"), "x", ("y", "zh", "zq")
    in_specs = (
        P(grp, col),
        P(grp, (row, *col)),
        P(col, row),
        P(row, grp, col),
        P(grp, None),
    )
    return jax.shard_map(
        per_device, mesh=fine, in_specs=in_specs, out_specs=P(col, row), check_vma=False
    )
```

```python
import jax
import jax.numpy as jnp
from jax import lax
from jax.experimental import pallas as pl
from jax.experimental.pallas import tpu as pltpu
from jax.sharding import Mesh, PartitionSpec as P

LEN = 96
VALID = 144
FEAT = 224
WIDE = 256
BF = jnp.bfloat16
F32 = jnp.float32
PLANE = ("zhi", "core", "y", "zh", "zq")
PARAMS = pltpu.CompilerParams(vmem_limit_bytes=16 << 20)


def to_basis(flip):
    def place(zhi, core, y, zlo):
        return ((zhi * 2 + core) * 4 + y) * 8 + zlo

    pairs = []
    for zhi in range(2):
        for core in range(2):
            for y in range(4):
                for z in range(8):
                    to = 7 - z if zhi != y >> 1 else z
                    there = place(y >> 1, zhi, core * 2 + (y & 1), to ^ flip)
                    pairs.append((place(zhi, core, y, z), there))
    return pairs


def exchange(x, axis):
    return lax.all_to_all(x, axis, 0, 0, tiled=True)


def everywhere(x, axis):
    return exchange(jnp.broadcast_to(x[None], (lax.axis_size(axis),) + x.shape), axis)


def swap(x, axis):
    return lax.ppermute(x, axis, [(0, 1), (1, 0)])


def across(left, right):
    return lax.dot_general(left, right, (((1,), (1,)), ((), ())), preferred_element_type=F32)


def chosen(first):
    slot = lax.broadcasted_iota(jnp.int32, (VALID, 2 * LEN), 0)
    line = lax.broadcasted_iota(jnp.int32, (VALID, 2 * LEN), 1)
    source = jnp.where(slot < first, slot, slot - first + LEN)
    return (source == line).astype(F32).astype(BF)


def pack_kernel(len_ref, grads_ref, out_ref):
    pick = chosen(len_ref[0, 0])
    out_ref[:, :FEAT] = jnp.dot(pick, grads_ref[...], preferred_element_type=F32).astype(BF)
    out_ref[:, FEAT:] = jnp.zeros((VALID, WIDE - FEAT), BF)


def inputs_kernel(where_ref, acts_ref, basis_ref, *out_refs):
    pick = chosen(where_ref[2])
    lines = jnp.dot(pick, acts_ref[...], preferred_element_type=F32).astype(BF)
    for k in range(4):
        at = pl.multiple_of((where_ref[5] ^ k) * WIDE, WIDE)
        out_refs[k][...] = jnp.dot(
            lines, basis_ref[:, pl.ds(at, WIDE)], preferred_element_type=F32
        ).astype(BF)


def join_kernel(near_ref, far_ref, *refs):
    parts, out_ref = refs[:4], refs[4]
    total = parts[0][...].astype(F32)
    for k in range(1, 4):
        total += parts[k][...].astype(F32)
    total = total.astype(BF)
    for d in range(4):
        for w, ref in enumerate((near_ref, far_ref)):
            at = d * 64 + w * 32
            out_ref[d, w] = jnp.concatenate([ref[:, :FEAT], total[:, at : at + 32]], axis=1)


def sort_kernel(where_ref, both_ref, out_ref, in_ref):
    zh, mirrored = where_ref[0], where_ref[1]
    for f in range(8):
        at = jnp.where(mirrored == 1, 7 - f, f)
        far = (at // 4 != zh).astype(jnp.int32)
        out_ref[:, f * FEAT : (f + 1) * FEAT] = both_ref[at % 4, far][:, :FEAT]
    sums = []
    for w in range(2):
        total = both_ref[0, w][:, FEAT:].astype(F32)
        for q in range(1, 4):
            total += both_ref[q, w][:, FEAT:].astype(F32)
        sums.append(total)
    half = VALID // 2
    packed = jnp.concatenate([x[i : i + half] for i in (0, half) for x in sums], axis=1)
    count = jnp.full((8, 128), where_ref[2], jnp.int32).astype(F32).astype(BF)
    for copy in range(16):
        in_ref[copy, :half] = packed.astype(BF)
        in_ref[copy, half:] = count


def merge_kernel(parts_ref, spread_ref):
    out_ref = spread_ref.at[0]
    half = VALID // 2
    for zhi in range(2):
        for q in range(4):
            at = zhi * 8 + q
            total = parts_ref[at, :half].astype(F32) + parts_ref[at + 4, :half].astype(F32)
            total = total.astype(BF)
            out_ref[zhi, :half, q * 64 : q * 64 + 64] = total[:, :64]
            out_ref[zhi, half:VALID, q * 64 : q * 64 + 64] = total[:, 64:]
        for h in range(2):
            out_ref[zhi, VALID:, h * 128 : h * 128 + 128] = parts_ref[zhi * 8, half:]
    for copy in range(1, 4):
        spread_ref[copy] = out_ref[...]


def project_kernel(where_ref, a_ref, b_ref, c_ref, d_ref, own_ref, other_ref, out_ref):
    yh, same = where_ref[7], where_ref[3] == where_ref[6]
    for left_ref, right_ref, t in ((a_ref, b_ref, yh), (c_ref, d_ref, 1 - yh)):
        left, right = left_ref[...], right_ref[...]
        total = across(jnp.where(same, left, right), own_ref[...])
        total += across(jnp.where(same, right, left), other_ref[...])
        for h in range(2):
            out_ref[2 * t + h] = total[h * 72 : (h + 1) * 72].astype(BF)


def sum_kernel(parts_ref, out_ref):
    total = parts_ref[0].astype(F32)
    for x in range(1, 4):
        total += parts_ref[x].astype(F32)
    out_ref[...] = total.astype(BF)


def spread_kernel(one_ref, two_ref, out_ref):
    total = (one_ref[...].astype(F32) + two_ref[...].astype(F32)).astype(BF)
    for x in range(4):
        out_ref[x] = total


def arrange_kernel(where_ref, own_ref, other_ref, out_ref, mask_ref):
    core = where_ref[3]
    slot = lax.broadcasted_iota(jnp.int32, (VALID, 128), 0).astype(F32)
    for zhi in range(2):
        for c in range(2):
            mine = core == c
            g = zhi * 2 + c
            for y in range(4):
                block = jnp.where(mine, own_ref[y, zhi], other_ref[y, zhi])
                out_ref[g, :, y * WIDE : (y + 1) * WIDE] = block[:VALID]
            count = block[VALID : VALID + 1, :128].astype(F32)
            mask_ref[g] = (slot < count).astype(F32).astype(BF)


def square_kernel(where_ref, own_ref, other_ref, in_ref, mask_ref, eig_ref, left_ref):
    core = where_ref[3]
    for g in range(4):
        mine = core == g // 2
        lines = jnp.where(mine, own_ref[g % 2], other_ref[g % 2])
        first = lines * mask_ref[g][:, :1]
        left_ref[2 * g] = first.T
        left_ref[2 * g + 1] = (lines - first).T
    rows, cols = 112, 256
    for o in range(448 // rows):
        for i in range(1024 // cols):
            total = jnp.zeros((rows, cols), F32)
            for s in range(8):
                block = jnp.dot(
                    left_ref[s, o * rows : (o + 1) * rows, :],
                    in_ref[s // 2, :, i * cols : (i + 1) * cols],
                    preferred_element_type=F32,
                )
                total += block * block
            eig_ref[o * rows : (o + 1) * rows, i * cols : (i + 1) * cols] = total / 768.0


def call(kernel, out, *args, scalars=1, scratch=()):
    single = not isinstance(out, (list, tuple))
    smem = pl.BlockSpec(memory_space=pltpu.SMEM)
    vmem = pl.BlockSpec(memory_space=pltpu.VMEM)
    outs = [out] if single else list(out)
    got = pl.pallas_call(
        kernel,
        in_specs=[smem] * scalars + [vmem] * (len(args) - scalars),
        out_specs=[vmem] * len(outs),
        out_shape=outs,
        scratch_shapes=scratch,
        compiler_params=PARAMS,
    )(*args)
    return got[0] if single else got


def like(*shape, dtype=BF):
    return jax.ShapeDtypeStruct(shape, dtype)


def others(x, axis):
    n = lax.axis_size(axis)
    return [lax.ppermute(x, axis, [(i, i ^ k) for i in range(n)]) for k in range(1, n)]


def per_device(acts, grads, basis_in, basis_out, lengths):
    zhi, core, y, zh, zq = (lax.axis_index(a) for a in ("zhi", "core", "y", "zh", "zq"))
    crossed = (core != zhi).astype(jnp.int32)
    where = jnp.stack([zh, crossed, lengths[0, 0], core, zq, y, y & 1, y >> 1])
    lines = call(pack_kernel, like(VALID, WIDE), lengths, grads)
    near = lax.ppermute(lines, PLANE, to_basis(0))
    far = lax.ppermute(lines, PLANE, to_basis(4))
    partial = call(inputs_kernel, [like(VALID, WIDE)] * 4, where, acts, basis_in)
    partial = [partial[0]] + [
        lax.ppermute(partial[k], "y", [(i, i ^ k) for i in range(4)]) for k in (1, 2, 3)
    ]
    basis = basis_out[0].T
    cols = basis.shape[0]
    other_basis = swap(basis, "core")
    both = call(join_kernel, like(4, 2, VALID, WIDE), near, far, *partial, scalars=0)
    both = exchange(both, "zq")
    lines, ins = call(sort_kernel, [like(VALID, 8 * FEAT), like(16, 80, 128)], where, both)
    lines = [lines] + others(lines, "y")
    ins = exchange(ins, ("zhi", "zh", "zq"))
    ins = call(merge_kernel, like(4, 2, VALID + 8, WIDE), ins, scalars=0)
    ins = exchange(ins, "y")
    ins, lines = lax.optimization_barrier((ins, lines))
    part = call(project_kernel, like(4, 72, cols), where, *lines, basis, other_basis)
    part = exchange(part, "x")
    part = call(sum_kernel, like(72, cols), part, scalars=0)
    part, ins = lax.optimization_barrier((part, ins))
    other_ins = swap(ins, "core")
    part = call(spread_kernel, like(4, 72, cols), part, swap(part, "zhi"), scalars=0)
    part, ins, other_ins = lax.optimization_barrier((part, ins, other_ins))
    outs = exchange(part, "x").reshape(2, VALID, cols)
    ins, masks = call(
        arrange_kernel,
        [like(4, VALID, 1024), like(4, VALID, 128)],
        where,
        ins,
        other_ins,
    )
    return call(
        square_kernel,
        like(cols, 1024, dtype=F32),
        where,
        outs,
        swap(outs, "core"),
        ins,
        masks,
        scratch=[pltpu.VMEM((8, cols, VALID), BF)],
    )


def solution(mesh):
    axes = ("zhi", "core", "x", "y", "zh", "zq")
    fine = Mesh(mesh.devices.reshape(2, 2, 4, 4, 2, 4), axes)
    grp, row, col = ("zhi", "core"), "x", ("y", "zh", "zq")
    in_specs = (
        P(grp, col),
        P(grp, (row, *col)),
        P(col, row),
        P(row, grp, col),
        P(grp, None),
    )
    return jax.shard_map(
        per_device, mesh=fine, in_specs=in_specs, out_specs=P(col, row), check_vma=False
    )
```

```python
import jax
import jax.numpy as jnp
from jax import lax
from jax.experimental import pallas as pl
from jax.experimental.pallas import tpu as pltpu
from jax.sharding import Mesh, PartitionSpec as P

LEN = 96
VALID = 144
FEAT = 224
WIDE = 256
BF = jnp.bfloat16
F32 = jnp.float32
HINT = pl.CostEstimate(flops=int(5e9), bytes_accessed=int(1e6), transcendentals=0)
LONG = pl.CostEstimate(flops=int(3e10), bytes_accessed=int(1e6), transcendentals=0)
PLANE = ("zhi", "core", "y", "zh", "zq")
PARAMS = pltpu.CompilerParams(vmem_limit_bytes=16 << 20)


def to_basis(flip):
    def place(zhi, core, y, zlo):
        return ((zhi * 2 + core) * 4 + y) * 8 + zlo

    pairs = []
    for zhi in range(2):
        for core in range(2):
            for y in range(4):
                for z in range(8):
                    to = 7 - z if zhi != y >> 1 else z
                    there = place(y >> 1, zhi, core * 2 + (y & 1), to ^ flip)
                    pairs.append((place(zhi, core, y, z), there))
    return pairs


def exchange(x, axis):
    return lax.all_to_all(x, axis, 0, 0, tiled=True)


def everywhere(x, axis):
    return exchange(jnp.broadcast_to(x[None], (lax.axis_size(axis),) + x.shape), axis)


def swap(x, axis):
    return lax.ppermute(x, axis, [(0, 1), (1, 0)])


def across(left, right):
    return lax.dot_general(left, right, (((1,), (1,)), ((), ())), preferred_element_type=F32)


def chosen(first):
    slot = lax.broadcasted_iota(jnp.int32, (VALID, 2 * LEN), 0)
    line = lax.broadcasted_iota(jnp.int32, (VALID, 2 * LEN), 1)
    source = jnp.where(slot < first, slot, slot - first + LEN)
    return (source == line).astype(F32).astype(BF)


def pack_kernel(len_ref, grads_ref, out_ref):
    pick = chosen(len_ref[0, 0])
    out_ref[:, :FEAT] = jnp.dot(pick, grads_ref[...], preferred_element_type=F32).astype(BF)
    out_ref[:, FEAT:] = jnp.zeros((VALID, WIDE - FEAT), BF)


def inputs_kernel(where_ref, acts_ref, basis_ref, out_ref):
    pick = chosen(where_ref[2])
    lines = jnp.dot(pick, acts_ref[...], preferred_element_type=F32).astype(BF)
    for y in range(4):
        out_ref[y] = jnp.dot(
            lines, basis_ref[:, y * WIDE : (y + 1) * WIDE], preferred_element_type=F32
        ).astype(BF)


def pair_kernel(near_ref, far_ref, out_ref):
    out_ref[0] = near_ref[...]
    out_ref[1] = far_ref[...]


def join_kernel(pair_ref, parts_ref, out_ref):
    total = parts_ref[0].astype(F32)
    for y in range(1, 4):
        total += parts_ref[y].astype(F32)
    total = total.astype(BF)
    for d in range(4):
        for w in range(2):
            at = d * 64 + w * 32
            out_ref[d, w] = jnp.concatenate(
                [pair_ref[w][:, :FEAT], total[:, at : at + 32]], axis=1
            )


def sort_kernel(where_ref, both_ref, out_ref, in_ref):
    zh, mirrored = where_ref[0], where_ref[1]
    for f in range(8):
        at = jnp.where(mirrored == 1, 7 - f, f)
        far = (at // 4 != zh).astype(jnp.int32)
        out_ref[:, f * FEAT : (f + 1) * FEAT] = both_ref[at % 4, far][:, :FEAT]
    sums = []
    for w in range(2):
        total = both_ref[0, w][:, FEAT:].astype(F32)
        for q in range(1, 4):
            total += both_ref[q, w][:, FEAT:].astype(F32)
        sums.append(total)
    half = VALID // 2
    packed = jnp.concatenate([x[i : i + half] for i in (0, half) for x in sums], axis=1)
    count = jnp.full((8, 128), where_ref[2], jnp.int32).astype(F32).astype(BF)
    for copy in range(16):
        in_ref[copy, :half] = packed.astype(BF)
        in_ref[copy, half:] = count


def merge_kernel(parts_ref, spread_ref):
    out_ref = spread_ref.at[0]
    half = VALID // 2
    for zhi in range(2):
        for q in range(4):
            at = zhi * 8 + q
            total = parts_ref[at, :half].astype(F32) + parts_ref[at + 4, :half].astype(F32)
            total = total.astype(BF)
            out_ref[zhi, :half, q * 64 : q * 64 + 64] = total[:, :64]
            out_ref[zhi, half:VALID, q * 64 : q * 64 + 64] = total[:, 64:]
        for h in range(2):
            out_ref[zhi, VALID:, h * 128 : h * 128 + 128] = parts_ref[zhi * 8, half:]
    for copy in range(1, 4):
        spread_ref[copy] = out_ref[...]


def project_kernel(where_ref, a_ref, b_ref, c_ref, d_ref, own_ref, other_ref, out_ref):
    yh, same = where_ref[7], where_ref[3] == where_ref[6]
    for left_ref, right_ref, t in ((a_ref, b_ref, yh), (c_ref, d_ref, 1 - yh)):
        left, right = left_ref[...], right_ref[...]
        total = across(jnp.where(same, left, right), own_ref[...])
        total += across(jnp.where(same, right, left), other_ref[...])
        for h in range(2):
            out_ref[2 * t + h] = total[h * 72 : (h + 1) * 72].astype(BF)


def sum_kernel(parts_ref, out_ref):
    total = parts_ref[0].astype(F32)
    for x in range(1, 4):
        total += parts_ref[x].astype(F32)
    out_ref[...] = total.astype(BF)


def spread_kernel(one_ref, two_ref, out_ref):
    total = (one_ref[...].astype(F32) + two_ref[...].astype(F32)).astype(BF)
    for x in range(4):
        out_ref[x] = total


def arrange_kernel(where_ref, own_ref, other_ref, out_ref, mask_ref):
    core = where_ref[3]
    slot = lax.broadcasted_iota(jnp.int32, (VALID, 128), 0).astype(F32)
    for zhi in range(2):
        for c in range(2):
            mine = core == c
            g = zhi * 2 + c
            for y in range(4):
                block = jnp.where(mine, own_ref[y, zhi], other_ref[y, zhi])
                out_ref[g, :, y * WIDE : (y + 1) * WIDE] = block[:VALID]
            count = block[VALID : VALID + 1, :128].astype(F32)
            mask_ref[g] = (slot < count).astype(F32).astype(BF)


def square_kernel(where_ref, own_ref, other_ref, in_ref, mask_ref, eig_ref, left_ref):
    core = where_ref[3]
    for g in range(4):
        mine = core == g // 2
        lines = jnp.where(mine, own_ref[g % 2], other_ref[g % 2])
        first = lines * mask_ref[g][:, :1]
        left_ref[2 * g] = first.T
        left_ref[2 * g + 1] = (lines - first).T
    rows, cols = 112, 256
    for o in range(448 // rows):
        for i in range(1024 // cols):
            total = jnp.zeros((rows, cols), F32)
            for s in range(8):
                block = jnp.dot(
                    left_ref[s, o * rows : (o + 1) * rows, :],
                    in_ref[s // 2, :, i * cols : (i + 1) * cols],
                    preferred_element_type=F32,
                )
                total += block * block
            eig_ref[o * rows : (o + 1) * rows, i * cols : (i + 1) * cols] = total / 768.0


def call(kernel, out, *args, scalars=1, scratch=(), cost=None):
    single = not isinstance(out, (list, tuple))
    smem = pl.BlockSpec(memory_space=pltpu.SMEM)
    vmem = pl.BlockSpec(memory_space=pltpu.VMEM)
    outs = [out] if single else list(out)
    got = pl.pallas_call(
        kernel,
        in_specs=[smem] * scalars + [vmem] * (len(args) - scalars),
        out_specs=[vmem] * len(outs),
        out_shape=outs,
        scratch_shapes=scratch,
        cost_estimate=cost,
        compiler_params=PARAMS,
    )(*args)
    return got[0] if single else got


def like(*shape, dtype=BF):
    return jax.ShapeDtypeStruct(shape, dtype)


def others(x, axis):
    n = lax.axis_size(axis)
    return [lax.ppermute(x, axis, [(i, i ^ k) for i in range(n)]) for k in range(1, n)]


def per_device(acts, grads, basis_in, basis_out, lengths):
    zhi, core, y, zh, zq = (lax.axis_index(a) for a in ("zhi", "core", "y", "zh", "zq"))
    crossed = (core != zhi).astype(jnp.int32)
    where = jnp.stack([zh, crossed, lengths[0, 0], core, zq, y, y & 1, y >> 1])
    lines = call(pack_kernel, like(VALID, WIDE), lengths, grads)
    near = lax.ppermute(lines, PLANE, to_basis(0))
    far = lax.ppermute(lines, PLANE, to_basis(4))
    partial = call(inputs_kernel, like(4, VALID, WIDE), where, acts, basis_in)
    partial = exchange(partial, "y")
    basis = basis_out[0].T
    cols = basis.shape[0]
    other_basis = swap(basis, "core")
    both = call(pair_kernel, like(2, VALID, WIDE), near, far, scalars=0, cost=HINT)
    both = call(join_kernel, like(4, 2, VALID, WIDE), both, partial, scalars=0)
    both = exchange(both, "zq")
    lines, ins = call(sort_kernel, [like(VALID, 8 * FEAT), like(16, 80, 128)], where, both)
    lines = [lines] + others(lines, "y")
    ins = exchange(ins, ("zhi", "zh", "zq"))
    part = call(project_kernel, like(4, 72, cols), where, *lines, basis, other_basis, cost=LONG)
    part, ins = lax.optimization_barrier((part, ins))
    ins = call(merge_kernel, like(4, 2, VALID + 8, WIDE), ins, scalars=0)
    part = exchange(part, "x")
    part = call(sum_kernel, like(72, cols), part, scalars=0)
    part, ins = lax.optimization_barrier((part, ins))
    ins = exchange(ins, "y")
    part = call(spread_kernel, like(4, 72, cols), part, swap(part, "zhi"), scalars=0, cost=HINT)
    part, ins = lax.optimization_barrier((part, ins))
    other_ins = swap(ins, "core")
    outs = exchange(part, "x").reshape(2, VALID, cols)
    ins, masks = call(
        arrange_kernel,
        [like(4, VALID, 1024), like(4, VALID, 128)],
        where,
        ins,
        other_ins,
    )
    return call(
        square_kernel,
        like(cols, 1024, dtype=F32),
        where,
        outs,
        swap(outs, "core"),
        ins,
        masks,
        scratch=[pltpu.VMEM((8, cols, VALID), BF)],
    )


def solution(mesh):
    axes = ("zhi", "core", "x", "y", "zh", "zq")
    fine = Mesh(mesh.devices.reshape(2, 2, 4, 4, 2, 4), axes)
    grp, row, col = ("zhi", "core"), "x", ("y", "zh", "zq")
    in_specs = (
        P(grp, col),
        P(grp, (row, *col)),
        P(col, row),
        P(row, grp, col),
        P(grp, None),
    )
    return jax.shard_map(
        per_device, mesh=fine, in_specs=in_specs, out_specs=P(col, row), check_vma=False
    )
```

```python
import jax
import jax.numpy as jnp
from jax import lax
from jax.experimental import pallas as pl
from jax.experimental.pallas import tpu as pltpu
from jax.sharding import Mesh, PartitionSpec as P

LEN = 96
VALID = 144
FEAT = 224
WIDE = 256
BF = jnp.bfloat16
F32 = jnp.float32
HINT = pl.CostEstimate(flops=int(5e9), bytes_accessed=int(1e6), transcendentals=0)
LONG = pl.CostEstimate(flops=int(3e10), bytes_accessed=int(1e6), transcendentals=0)
PLANE = ("zhi", "core", "y", "zh", "zq")
PARAMS = pltpu.CompilerParams(vmem_limit_bytes=16 << 20)


def to_basis(far):
    def place(zhi, core, y, zlo):
        return ((zhi * 2 + core) * 4 + y) * 8 + zlo

    pairs = []
    for zhi in range(2):
        for core in range(2):
            for y in range(4):
                for z in range(8):
                    crossed = zhi != y >> 1
                    to = (z ^ 3 if far else z ^ 4) if crossed else (z ^ 4 if far else z)
                    there = place(y >> 1, zhi, core * 2 + (y & 1), to)
                    pairs.append((place(zhi, core, y, z), there))
    return pairs


def exchange(x, axis):
    return lax.all_to_all(x, axis, 0, 0, tiled=True)


def everywhere(x, axis):
    return exchange(jnp.broadcast_to(x[None], (lax.axis_size(axis),) + x.shape), axis)


def swap(x, axis):
    return lax.ppermute(x, axis, [(0, 1), (1, 0)])


def across(left, right):
    return lax.dot_general(left, right, (((1,), (1,)), ((), ())), preferred_element_type=F32)


def chosen(first):
    slot = lax.broadcasted_iota(jnp.int32, (VALID, 2 * LEN), 0)
    line = lax.broadcasted_iota(jnp.int32, (VALID, 2 * LEN), 1)
    source = jnp.where(slot < first, slot, slot - first + LEN)
    return (source == line).astype(F32).astype(BF)


def pack_kernel(len_ref, grads_ref, out_ref):
    pick = chosen(len_ref[0, 0])
    out_ref[:, :FEAT] = jnp.dot(pick, grads_ref[...], preferred_element_type=F32).astype(BF)
    out_ref[:, FEAT:] = jnp.zeros((VALID, WIDE - FEAT), BF)


def inputs_kernel(where_ref, acts_ref, basis_ref, out_ref):
    pick = chosen(where_ref[2])
    lines = jnp.dot(pick, acts_ref[...], preferred_element_type=F32).astype(BF)
    for y in range(4):
        out_ref[y] = jnp.dot(
            lines, basis_ref[:, y * WIDE : (y + 1) * WIDE], preferred_element_type=F32
        ).astype(BF)


def pair_kernel(near_ref, far_ref, out_ref):
    out_ref[0] = near_ref[...]
    out_ref[1] = far_ref[...]


def join_kernel(pair_ref, parts_ref, out_ref):
    total = parts_ref[0].astype(F32)
    for y in range(1, 4):
        total += parts_ref[y].astype(F32)
    total = total.astype(BF)
    for d in range(4):
        for w in range(2):
            at = d * 64 + w * 32
            out_ref[d, w] = jnp.concatenate(
                [pair_ref[w][:, :FEAT], total[:, at : at + 32]], axis=1
            )


def sort_kernel(where_ref, both_ref, out_ref, in_ref):
    zh, crossed = where_ref[0], where_ref[1]
    for f in range(8):
        far = (jnp.int32(f // 4) != zh).astype(jnp.int32) ^ crossed
        at = (f % 4) ^ (3 * (far & crossed))
        out_ref[:, f * FEAT : (f + 1) * FEAT] = both_ref[at, far][:, :FEAT]
    sums = []
    for w in range(2):
        total = both_ref[0, w][:, FEAT:].astype(F32)
        for q in range(1, 4):
            total += both_ref[q, w][:, FEAT:].astype(F32)
        sums.append(total)
    half = VALID // 2
    packed = jnp.concatenate([x[i : i + half] for i in (0, half) for x in sums], axis=1)
    count = jnp.full((8, 128), where_ref[2], jnp.int32).astype(F32).astype(BF)
    for copy in range(16):
        in_ref[copy, :half] = packed.astype(BF)
        in_ref[copy, half:] = count


def merge_kernel(parts_ref, out_ref):
    half = VALID // 2
    for zhi in range(2):
        for q in range(4):
            at = zhi * 8 + q
            total = parts_ref[at, :half].astype(F32) + parts_ref[at + 4, :half].astype(F32)
            total = total.astype(BF)
            out_ref[zhi, :half, q * 64 : q * 64 + 64] = total[:, :64]
            out_ref[zhi, half:VALID, q * 64 : q * 64 + 64] = total[:, 64:]
        for h in range(2):
            out_ref[zhi, VALID:, h * 128 : h * 128 + 128] = parts_ref[zhi * 8, half:]


def project_kernel(where_ref, a_ref, b_ref, c_ref, d_ref, own_ref, other_ref, out_ref, held):
    yh, same = where_ref[7], where_ref[3] == where_ref[6]
    for left_ref, right_ref, t in ((a_ref, b_ref, yh), (c_ref, d_ref, 1 - yh)):
        left, right = left_ref[...], right_ref[...]
        held[0, t] = jnp.where(same, left, right)
        held[1, t] = jnp.where(same, right, left)
    rows = (2 * VALID, held.shape[3])
    total = across(held[0].reshape(rows), own_ref[...])
    total += across(held[1].reshape(rows), other_ref[...])
    for h in range(4):
        out_ref[h] = total[h * 72 : (h + 1) * 72].astype(BF)


def sum_kernel(parts_ref, out_ref):
    total = parts_ref[0].astype(F32)
    for x in range(1, 4):
        total += parts_ref[x].astype(F32)
    out_ref[...] = total.astype(BF)


def spread_kernel(one_ref, two_ref, out_ref):
    total = (one_ref[...].astype(F32) + two_ref[...].astype(F32)).astype(BF)
    for x in range(4):
        out_ref[x] = total


def arrange_kernel(where_ref, own_ref, other_ref, out_ref, mask_ref):
    core = where_ref[3]
    slot = lax.broadcasted_iota(jnp.int32, (8, VALID), 1).astype(F32)
    for zhi in range(2):
        for c in range(2):
            mine = core == c
            g = zhi * 2 + c
            for y in range(4):
                k = y ^ where_ref[5]
                block = jnp.where(mine, own_ref[k, zhi], other_ref[k, zhi])
                out_ref[g, :, y * WIDE : (y + 1) * WIDE] = block[:VALID]
            count = block[VALID:, :VALID].astype(F32)
            mask_ref[g] = (slot < count).astype(F32).astype(BF)


def left_kernel(lines_ref, left_ref):
    for t in range(2):
        left_ref[t] = lines_ref[t].T


def square_kernel(where_ref, own_ref, other_ref, in_ref, mask_ref, eig_ref, left_ref):
    core = where_ref[3]
    for t in range(2):
        for at, lines in (
            (2 * core + t, own_ref[t]),
            (2 * (1 - core) + t, other_ref[t].T),
        ):
            first = lines * mask_ref[at][:1]
            left_ref[2 * at] = first
            left_ref[2 * at + 1] = lines - first
    rows, cols = 224, 256
    for i in range(1024 // cols):
        for o in range(448 // rows):
            total = jnp.zeros((rows, cols), F32)
            for s in range(8):
                block = jnp.dot(
                    left_ref[s, o * rows : (o + 1) * rows, :],
                    in_ref[s // 2, :, i * cols : (i + 1) * cols],
                    preferred_element_type=F32,
                )
                total += block * block
            eig_ref[o * rows : (o + 1) * rows, i * cols : (i + 1) * cols] = total / 768.0


def call(kernel, out, *args, scalars=1, scratch=(), cost=None):
    single = not isinstance(out, (list, tuple))
    smem = pl.BlockSpec(memory_space=pltpu.SMEM)
    vmem = pl.BlockSpec(memory_space=pltpu.VMEM)
    outs = [out] if single else list(out)
    got = pl.pallas_call(
        kernel,
        in_specs=[smem] * scalars + [vmem] * (len(args) - scalars),
        out_specs=[vmem] * len(outs),
        out_shape=outs,
        scratch_shapes=scratch,
        cost_estimate=cost,
        compiler_params=PARAMS,
    )(*args)
    return got[0] if single else got


def like(*shape, dtype=BF):
    return jax.ShapeDtypeStruct(shape, dtype)


def others(x, axis):
    n = lax.axis_size(axis)
    sent = {k: lax.ppermute(x, axis, [(i, i ^ k) for i in range(n)]) for k in (1, 3, 2)}
    return [sent[k] for k in (1, 2, 3)]


def per_device(acts, grads, basis_in, basis_out, lengths):
    zhi, core, y, zh, zq = (lax.axis_index(a) for a in ("zhi", "core", "y", "zh", "zq"))
    crossed = (core != zhi).astype(jnp.int32)
    where = jnp.stack([zh, crossed, lengths[0, 0], core, zq, y, y & 1, y >> 1])
    lines = call(pack_kernel, like(VALID, WIDE), lengths, grads)
    near = lax.ppermute(lines, PLANE, to_basis(False))
    far = lax.ppermute(lines, PLANE, to_basis(True))
    partial = call(inputs_kernel, like(4, VALID, WIDE), where, acts, basis_in)
    partial = exchange(partial, "y")
    basis = basis_out[0].T
    cols = basis.shape[0]
    other_basis = swap(basis, "core")
    both = call(pair_kernel, like(2, VALID, WIDE), near, far, scalars=0, cost=HINT)
    both = call(join_kernel, like(4, 2, VALID, WIDE), both, partial, scalars=0)
    both = exchange(both, "zq")
    lines, ins = call(sort_kernel, [like(VALID, 8 * FEAT), like(16, 80, 128)], where, both)
    lines = [lines] + others(lines, "y")
    ins = exchange(ins, ("zhi", "zh", "zq"))
    part = call(
        project_kernel,
        like(4, 72, cols),
        where,
        *lines,
        basis,
        other_basis,
        cost=LONG,
        scratch=[pltpu.VMEM((2, 2, VALID, 8 * FEAT), BF)],
    )
    part, ins = lax.optimization_barrier((part, ins))
    ins = call(merge_kernel, like(2, VALID + 8, WIDE), ins, scalars=0)
    part = exchange(part, "x")
    part = call(sum_kernel, like(72, cols), part, scalars=0)
    part, ins = lax.optimization_barrier((part, ins))
    ins = [ins] + others(ins, "y")
    part = call(spread_kernel, like(4, 72, cols), part, swap(part, "zhi"), scalars=0, cost=HINT)
    part, ins = lax.optimization_barrier((part, ins))
    ins = jnp.stack(ins)
    other_ins = swap(ins, "core")
    outs = exchange(part, "x").reshape(2, VALID, cols)
    ins, masks = call(
        arrange_kernel,
        [like(4, VALID, 1024), like(4, 8, VALID)],
        where,
        ins,
        other_ins,
    )
    left = call(left_kernel, like(2, cols, VALID), outs, scalars=0, cost=HINT)
    return call(
        square_kernel,
        like(cols, 1024, dtype=F32),
        where,
        left,
        swap(outs, "core"),
        ins,
        masks,
        scratch=[pltpu.VMEM((8, cols, VALID), BF)],
    )


def solution(mesh):
    axes = ("zhi", "core", "x", "y", "zh", "zq")
    fine = Mesh(mesh.devices.reshape(2, 2, 4, 4, 2, 4), axes)
    grp, row, col = ("zhi", "core"), "x", ("y", "zh", "zq")
    in_specs = (
        P(grp, col),
        P(grp, (row, *col)),
        P(col, row),
        P(row, grp, col),
        P(grp, None),
    )
    return jax.shard_map(
        per_device, mesh=fine, in_specs=in_specs, out_specs=P(col, row), check_vma=False
    )
```

```python
import jax
import jax.numpy as jnp
from jax import lax
from jax.experimental import pallas as pl
from jax.experimental.pallas import tpu as pltpu
from jax.sharding import Mesh, PartitionSpec as P

LEN = 96
VALID = 144
FEAT = 224
WIDE = 256
BF = jnp.bfloat16
F32 = jnp.float32
HINT = pl.CostEstimate(flops=int(5e9), bytes_accessed=int(1e6), transcendentals=0)
LONG = pl.CostEstimate(flops=int(3e10), bytes_accessed=int(1e6), transcendentals=0)
PLANE = ("zhi", "core", "y", "zh", "zq")
PARAMS = pltpu.CompilerParams(vmem_limit_bytes=16 << 20)


def to_basis(far):
    def place(zhi, core, y, zlo):
        return ((zhi * 2 + core) * 4 + y) * 8 + zlo

    pairs = []
    for zhi in range(2):
        for core in range(2):
            for y in range(4):
                for z in range(8):
                    crossed = zhi != y >> 1
                    to = (z ^ 3 if far else z ^ 4) if crossed else (z ^ 4 if far else z)
                    there = place(y >> 1, zhi, core * 2 + (y & 1), to)
                    pairs.append((place(zhi, core, y, z), there))
    return pairs


def exchange(x, axis):
    return lax.all_to_all(x, axis, 0, 0, tiled=True)


def everywhere(x, axis):
    return exchange(jnp.broadcast_to(x[None], (lax.axis_size(axis),) + x.shape), axis)


def swap(x, axis):
    return lax.ppermute(x, axis, [(0, 1), (1, 0)])


def across(left, right):
    return lax.dot_general(left, right, (((1,), (1,)), ((), ())), preferred_element_type=F32)


def chosen(first):
    slot = lax.broadcasted_iota(jnp.int32, (VALID, 2 * LEN), 0)
    line = lax.broadcasted_iota(jnp.int32, (VALID, 2 * LEN), 1)
    source = jnp.where(slot < first, slot, slot - first + LEN)
    return (source == line).astype(F32).astype(BF)


def start_kernel(len_ref, grads_hbm, acts_hbm, basis_hbm, lines_ref, part_ref, *scratch):
    held, sems = scratch[:3], scratch[3:]
    copies = [
        pltpu.make_async_copy(source, ref, sem)
        for source, ref, sem in zip((acts_hbm, basis_hbm, grads_hbm), held, sems)
    ]
    for copy in copies:
        copy.start()
    acts_ref, basis_ref, grads_ref = held
    pick = chosen(len_ref[0, 0])
    copies[0].wait()
    lines = jnp.dot(pick, acts_ref[...], preferred_element_type=F32).astype(BF)
    copies[1].wait()
    for y in range(4):
        part_ref[y] = jnp.dot(
            lines, basis_ref[:, y * WIDE : (y + 1) * WIDE], preferred_element_type=F32
        ).astype(BF)
    copies[2].wait()
    lines_ref[:, :FEAT] = jnp.dot(pick, grads_ref[...], preferred_element_type=F32).astype(BF)
    lines_ref[:, FEAT:] = jnp.zeros((VALID, WIDE - FEAT), BF)


def join_kernel(near_ref, far_ref, parts_ref, out_ref):
    total = parts_ref[0].astype(F32)
    for y in range(1, 4):
        total += parts_ref[y].astype(F32)
    total = total.astype(BF)
    for d in range(4):
        for w, ref in enumerate((near_ref, far_ref)):
            at = d * 64 + w * 32
            out_ref[d, w] = jnp.concatenate([ref[:, :FEAT], total[:, at : at + 32]], axis=1)


def sort_kernel(where_ref, both_ref, out_ref, in_ref):
    zh, crossed = where_ref[0], where_ref[1]
    for f in range(8):
        far = (jnp.int32(f // 4) != zh).astype(jnp.int32) ^ crossed
        at = (f % 4) ^ (3 * (far & crossed))
        out_ref[:, f * FEAT : (f + 1) * FEAT] = both_ref[at, far][:, :FEAT]
    sums = []
    for w in range(2):
        total = both_ref[0, w][:, FEAT:].astype(F32)
        for q in range(1, 4):
            total += both_ref[q, w][:, FEAT:].astype(F32)
        sums.append(total)
    half = VALID // 2
    packed = jnp.concatenate([x[i : i + half] for i in (0, half) for x in sums], axis=1)
    count = jnp.full((8, 128), where_ref[2], jnp.int32).astype(F32).astype(BF)
    for copy in range(16):
        in_ref[copy, :half] = packed.astype(BF)
        in_ref[copy, half:] = count


def merge_kernel(parts_ref, out_ref):
    half = VALID // 2
    for zhi in range(2):
        for q in range(4):
            at = zhi * 8 + q
            total = parts_ref[at, :half].astype(F32) + parts_ref[at + 4, :half].astype(F32)
            total = total.astype(BF)
            out_ref[zhi, :half, q * 64 : q * 64 + 64] = total[:, :64]
            out_ref[zhi, half:VALID, q * 64 : q * 64 + 64] = total[:, 64:]
        for h in range(2):
            out_ref[zhi, VALID:, h * 128 : h * 128 + 128] = parts_ref[zhi * 8, half:]


def project_kernel(where_ref, a_ref, b_ref, c_ref, d_ref, own_ref, other_ref, out_ref, held):
    yh, same = where_ref[7], where_ref[3] == where_ref[6]
    for left_ref, right_ref, t in ((a_ref, b_ref, yh), (c_ref, d_ref, 1 - yh)):
        left, right = left_ref[...], right_ref[...]
        held[0, t] = jnp.where(same, left, right)
        held[1, t] = jnp.where(same, right, left)
    rows = (2 * VALID, held.shape[3])
    total = across(held[0].reshape(rows), own_ref[...])
    total += across(held[1].reshape(rows), other_ref[...])
    for h in range(4):
        out_ref[h] = total[h * 72 : (h + 1) * 72].astype(BF)


def sum_kernel(parts_ref, out_ref):
    total = parts_ref[0].astype(F32)
    for x in range(1, 4):
        total += parts_ref[x].astype(F32)
    out_ref[...] = total.astype(BF)


def spread_kernel(one_ref, two_ref, out_ref):
    total = (one_ref[...].astype(F32) + two_ref[...].astype(F32)).astype(BF)
    for x in range(4):
        out_ref[x] = total


def arrange_kernel(where_ref, own_ref, other_ref, out_ref, mask_ref):
    core = where_ref[3]
    slot = lax.broadcasted_iota(jnp.int32, (8, VALID), 1).astype(F32)
    for zhi in range(2):
        for c in range(2):
            mine = core == c
            g = zhi * 2 + c
            for y in range(4):
                k = y ^ where_ref[5]
                block = jnp.where(mine, own_ref[k, zhi], other_ref[k, zhi])
                out_ref[g, :, y * WIDE : (y + 1) * WIDE] = block[:VALID]
            count = block[VALID:, :VALID].astype(F32)
            mask_ref[g] = (slot < count).astype(F32).astype(BF)


def left_kernel(lines_ref, left_ref):
    for t in range(2):
        left_ref[t] = lines_ref[t].T


def square_kernel(where_ref, own_ref, other_ref, in_ref, mask_ref, eig_ref, left_ref):
    core = where_ref[3]
    for t in range(2):
        for at, lines in (
            (2 * core + t, own_ref[t]),
            (2 * (1 - core) + t, other_ref[t].T),
        ):
            first = lines * mask_ref[at][:1]
            left_ref[2 * at] = first
            left_ref[2 * at + 1] = lines - first
    rows, cols = 224, 256
    for i in range(1024 // cols):
        for o in range(448 // rows):
            total = jnp.zeros((rows, cols), F32)
            for s in range(8):
                block = jnp.dot(
                    left_ref[s, o * rows : (o + 1) * rows, :],
                    in_ref[s // 2, :, i * cols : (i + 1) * cols],
                    preferred_element_type=F32,
                )
                total += block * block
            eig_ref[o * rows : (o + 1) * rows, i * cols : (i + 1) * cols] = total / 768.0


def call(kernel, out, *args, scalars=1, scratch=(), cost=None):
    single = not isinstance(out, (list, tuple))
    smem = pl.BlockSpec(memory_space=pltpu.SMEM)
    vmem = pl.BlockSpec(memory_space=pltpu.VMEM)
    outs = [out] if single else list(out)
    got = pl.pallas_call(
        kernel,
        in_specs=[smem] * scalars + [vmem] * (len(args) - scalars),
        out_specs=[vmem] * len(outs),
        out_shape=outs,
        scratch_shapes=scratch,
        cost_estimate=cost,
        compiler_params=PARAMS,
    )(*args)
    return got[0] if single else got


def like(*shape, dtype=BF):
    return jax.ShapeDtypeStruct(shape, dtype)


def others(x, axis):
    n = lax.axis_size(axis)
    sent = {k: lax.ppermute(x, axis, [(i, i ^ k) for i in range(n)]) for k in (1, 3, 2)}
    return [sent[k] for k in (1, 2, 3)]


def per_device(acts, grads, basis_in, basis_out, lengths):
    zhi, core, y, zh, zq = (lax.axis_index(a) for a in ("zhi", "core", "y", "zh", "zq"))
    crossed = (core != zhi).astype(jnp.int32)
    where = jnp.stack([zh, crossed, lengths[0, 0], core, zq, y, y & 1, y >> 1])
    lines, partial = pl.pallas_call(
        start_kernel,
        in_specs=[pl.BlockSpec(memory_space=pltpu.SMEM)] + [pl.BlockSpec(memory_space=pl.ANY)] * 3,
        out_specs=[pl.BlockSpec(memory_space=pltpu.VMEM)] * 2,
        out_shape=[like(VALID, WIDE), like(4, VALID, WIDE)],
        scratch_shapes=[pltpu.VMEM(x.shape, BF) for x in (acts, basis_in, grads)]
        + [pltpu.SemaphoreType.DMA] * 3,
        compiler_params=pltpu.CompilerParams(vmem_limit_bytes=60 << 20),
    )(lengths, grads, acts, basis_in)
    near = lax.ppermute(lines, PLANE, to_basis(False))
    far = lax.ppermute(lines, PLANE, to_basis(True))
    partial = exchange(partial, "y")
    basis = basis_out[0].T
    cols = basis.shape[0]
    other_basis = swap(basis, "core")
    both = call(join_kernel, like(4, 2, VALID, WIDE), near, far, partial, scalars=0)
    both = exchange(both, "zq")
    lines, ins = call(sort_kernel, [like(VALID, 8 * FEAT), like(16, 80, 128)], where, both)
    lines = [lines] + others(lines, "y")
    ins = exchange(ins, ("zhi", "zh", "zq"))
    part = call(
        project_kernel,
        like(4, 72, cols),
        where,
        *lines,
        basis,
        other_basis,
        cost=LONG,
        scratch=[pltpu.VMEM((2, 2, VALID, 8 * FEAT), BF)],
    )
    part, ins = lax.optimization_barrier((part, ins))
    ins = call(merge_kernel, like(2, VALID + 8, WIDE), ins, scalars=0)
    part = exchange(part, "x")
    part = call(sum_kernel, like(72, cols), part, scalars=0)
    part, ins = lax.optimization_barrier((part, ins))
    ins = [ins] + others(ins, "y")
    part = call(spread_kernel, like(4, 72, cols), part, swap(part, "zhi"), scalars=0, cost=HINT)
    ins = jnp.stack(ins)
    other_ins = swap(ins, "core")
    outs = exchange(part, "x").reshape(2, VALID, cols)
    ins, masks = call(
        arrange_kernel,
        [like(4, VALID, 1024), like(4, 8, VALID)],
        where,
        ins,
        other_ins,
    )
    left = call(left_kernel, like(2, cols, VALID), outs, scalars=0, cost=HINT)
    return call(
        square_kernel,
        like(cols, 1024, dtype=F32),
        where,
        left,
        swap(outs, "core"),
        ins,
        masks,
        scratch=[pltpu.VMEM((8, cols, VALID), BF)],
    )


def solution(mesh):
    axes = ("zhi", "core", "x", "y", "zh", "zq")
    fine = Mesh(mesh.devices.reshape(2, 2, 4, 4, 2, 4), axes)
    grp, row, col = ("zhi", "core"), "x", ("y", "zh", "zq")
    in_specs = (
        P(grp, col),
        P(grp, (row, *col)),
        P(col, row),
        P(row, grp, col),
        P(grp, None),
    )
    return jax.shard_map(
        per_device, mesh=fine, in_specs=in_specs, out_specs=P(col, row), check_vma=False
    )
```

```python
import jax
import jax.numpy as jnp
from jax import lax
from jax.experimental import pallas as pl
from jax.experimental.pallas import tpu as pltpu
from jax.sharding import Mesh, PartitionSpec as P

LEN = 96
VALID = 144
FEAT = 224
WIDE = 256
BF = jnp.bfloat16
F32 = jnp.float32
HINT = pl.CostEstimate(flops=int(5e9), bytes_accessed=int(1e6), transcendentals=0)
LONG = pl.CostEstimate(flops=int(3e10), bytes_accessed=int(1e6), transcendentals=0)
PLANE = ("zhi", "core", "y", "zh", "zq")
PARAMS = pltpu.CompilerParams(vmem_limit_bytes=16 << 20)


def to_basis(far):
    def place(zhi, core, y, zlo):
        return ((zhi * 2 + core) * 4 + y) * 8 + zlo

    pairs = []
    for zhi in range(2):
        for core in range(2):
            for y in range(4):
                for z in range(8):
                    crossed = zhi != y >> 1
                    to = (z ^ 3 if far else z ^ 4) if crossed else (z ^ 4 if far else z)
                    to_y = 2 * (core ^ (y >> 1)) + ((y & 1) ^ core)
                    there = place(y >> 1, zhi, to_y, to)
                    pairs.append((place(zhi, core, y, z), there))
    return pairs


def exchange(x, axis):
    return lax.all_to_all(x, axis, 0, 0, tiled=True)


def everywhere(x, axis):
    return exchange(jnp.broadcast_to(x[None], (lax.axis_size(axis),) + x.shape), axis)


def swap(x, axis):
    return lax.ppermute(x, axis, [(0, 1), (1, 0)])


def across(left, right):
    return lax.dot_general(left, right, (((1,), (1,)), ((), ())), preferred_element_type=F32)


def chosen(first):
    slot = lax.broadcasted_iota(jnp.int32, (VALID, 2 * LEN), 0)
    line = lax.broadcasted_iota(jnp.int32, (VALID, 2 * LEN), 1)
    source = jnp.where(slot < first, slot, slot - first + LEN)
    return (source == line).astype(F32).astype(BF)


def start_kernel(len_ref, grads_hbm, acts_hbm, basis_hbm, lines_ref, part_ref, *scratch):
    held, sems = scratch[:3], scratch[3:]
    copies = [
        pltpu.make_async_copy(source, ref, sem)
        for source, ref, sem in zip((acts_hbm, basis_hbm, grads_hbm), held, sems)
    ]
    for copy in copies:
        copy.start()
    acts_ref, basis_ref, grads_ref = held
    pick = chosen(len_ref[0, 0])
    copies[0].wait()
    lines = jnp.dot(pick, acts_ref[...], preferred_element_type=F32).astype(BF)
    copies[1].wait()
    for y in range(4):
        part_ref[y] = jnp.dot(
            lines, basis_ref[:, y * WIDE : (y + 1) * WIDE], preferred_element_type=F32
        ).astype(BF)
    copies[2].wait()
    lines_ref[:, :FEAT] = jnp.dot(pick, grads_ref[...], preferred_element_type=F32).astype(BF)
    lines_ref[:, FEAT:] = jnp.zeros((VALID, WIDE - FEAT), BF)


def join_kernel(near_ref, far_ref, parts_ref, out_ref):
    total = parts_ref[0].astype(F32)
    for y in range(1, 4):
        total += parts_ref[y].astype(F32)
    total = total.astype(BF)
    for d in range(4):
        for w, ref in enumerate((near_ref, far_ref)):
            at = d * 64 + w * 32
            out_ref[d, w] = jnp.concatenate([ref[:, :FEAT], total[:, at : at + 32]], axis=1)


def sort_kernel(where_ref, both_ref, out_ref):
    zh, crossed = where_ref[0], where_ref[1]
    for f in range(8):
        far = (jnp.int32(f // 4) != zh).astype(jnp.int32) ^ crossed
        at = (f % 4) ^ (3 * (far & crossed))
        out_ref[:, f * FEAT : (f + 1) * FEAT] = both_ref[at, far][:, :FEAT]


def pack_kernel(where_ref, both_ref, in_ref):
    sums = []
    for w in range(2):
        total = both_ref[0, w][:, FEAT:].astype(F32)
        for q in range(1, 4):
            total += both_ref[q, w][:, FEAT:].astype(F32)
        sums.append(total)
    half = VALID // 2
    packed = jnp.concatenate([x[i : i + half] for i in (0, half) for x in sums], axis=1)
    count = jnp.full((8, 128), where_ref[2], jnp.int32).astype(F32).astype(BF)
    for copy in range(16):
        in_ref[copy, :half] = packed.astype(BF)
        in_ref[copy, half:] = count


def merge_kernel(parts_ref, out_ref):
    half = VALID // 2
    for zhi in range(2):
        for q in range(4):
            at = zhi * 8 + q
            total = parts_ref[at, :half].astype(F32) + parts_ref[at + 4, :half].astype(F32)
            total = total.astype(BF)
            out_ref[zhi, :half, q * 64 : q * 64 + 64] = total[:, :64]
            out_ref[zhi, half:VALID, q * 64 : q * 64 + 64] = total[:, 64:]
        for h in range(2):
            out_ref[zhi, VALID:, h * 128 : h * 128 + 128] = parts_ref[zhi * 8, half:]


def project_kernel(
    where_ref, a_ref, b_ref, c_ref, d_ref, own_ref, other_ref, out_ref, held, total_ref
):
    step = pl.program_id(0)
    tokens, same = where_ref[7], where_ref[3] == where_ref[6]
    for left_ref, right_ref, t in ((a_ref, b_ref, tokens), (d_ref, c_ref, 1 - tokens)):
        left, right = left_ref[...], right_ref[...]
        held[0, t] = jnp.where(same, left, right)
        held[1, t] = jnp.where(same, right, left)
    rows = (2 * VALID, held.shape[3])
    total = across(held[0].reshape(rows), own_ref[...])
    total += across(held[1].reshape(rows), other_ref[...])

    @pl.when(step == 0)
    def _():
        total_ref[...] = total

    @pl.when(step > 0)
    def _():
        total_ref[...] += total

    @pl.when(step == pl.num_programs(0) - 1)
    def _():
        for h in range(4):
            out_ref[h] = total_ref[h * 72 : (h + 1) * 72].astype(BF)


def project(where, lines, basis, other_basis):
    cols, rows = basis.shape
    deep = rows // 2
    line = pl.BlockSpec((VALID, deep), lambda k: (0, k))
    rotated = pl.BlockSpec((cols, deep), lambda k: (0, k))
    return pl.pallas_call(
        project_kernel,
        grid=(rows // deep,),
        in_specs=[pl.BlockSpec(memory_space=pltpu.SMEM)] + [line] * 4 + [rotated] * 2,
        out_specs=pl.BlockSpec((4, 72, cols), lambda k: (0, 0, 0)),
        out_shape=like(4, 72, cols),
        scratch_shapes=[pltpu.VMEM((2, 2, VALID, deep), BF), pltpu.VMEM((2 * VALID, cols), F32)],
        compiler_params=PARAMS,
        cost_estimate=LONG,
    )(where, *lines, basis, other_basis)


def sum_kernel(parts_ref, out_ref):
    total = parts_ref[0].astype(F32)
    for x in range(1, 4):
        total += parts_ref[x].astype(F32)
    out_ref[...] = total.astype(BF)


def spread_kernel(one_ref, two_ref, out_ref):
    total = (one_ref[...].astype(F32) + two_ref[...].astype(F32)).astype(BF)
    for x in range(4):
        out_ref[x] = total


def arrange_kernel(where_ref, own_ref, other_ref, out_ref, mask_ref):
    core = where_ref[3]
    slot = lax.broadcasted_iota(jnp.int32, (8, VALID), 1).astype(F32)
    for zhi in range(2):
        for c in range(2):
            mine = core == c
            g = zhi * 2 + c
            for y in range(4):
                k = y ^ where_ref[5]
                block = jnp.where(mine, own_ref[k, zhi], other_ref[k, zhi])
                out_ref[g, :, y * WIDE : (y + 1) * WIDE] = block[:VALID]
            count = block[VALID:, :VALID].astype(F32)
            mask_ref[g] = (slot < count).astype(F32).astype(BF)


def left_kernel(lines_ref, left_ref):
    for t in range(2):
        left_ref[t] = lines_ref[t].T


def square_kernel(where_ref, own_ref, other_ref, in_ref, mask_ref, eig_ref, left_ref):
    core = where_ref[3]

    @pl.when(pl.program_id(0) == 0)
    def _():
        for t in range(2):
            for at, lines in (
                (2 * core + t, own_ref[t]),
                (2 * (1 - core) + t, other_ref[t].T),
            ):
                first = lines * mask_ref[at][:1]
                left_ref[2 * at] = first
                left_ref[2 * at + 1] = lines - first

    rows = 224
    for o in range(448 // rows):
        total = jnp.zeros((rows, eig_ref.shape[1]), F32)
        for s in range(8):
            block = jnp.dot(
                left_ref[s, o * rows : (o + 1) * rows, :],
                in_ref[s // 2],
                preferred_element_type=F32,
            )
            total += block * block
        eig_ref[o * rows : (o + 1) * rows] = total / 768.0


def squares(where, left, other, ins, masks):
    cols, wide, tile = left.shape[1], ins.shape[2], 256
    whole = lambda x: pl.BlockSpec(x.shape, lambda i: (0, 0, 0))
    return pl.pallas_call(
        square_kernel,
        grid=(wide // tile,),
        in_specs=[
            pl.BlockSpec(memory_space=pltpu.SMEM),
            whole(left),
            whole(other),
            pl.BlockSpec((4, VALID, tile), lambda i: (0, 0, i)),
            whole(masks),
        ],
        out_specs=pl.BlockSpec((cols, tile), lambda i: (0, i)),
        out_shape=like(cols, wide, dtype=F32),
        scratch_shapes=[pltpu.VMEM((8, cols, VALID), BF)],
        compiler_params=PARAMS,
    )(where, left, other, ins, masks)


def call(kernel, out, *args, scalars=1, scratch=(), cost=None):
    single = not isinstance(out, (list, tuple))
    smem = pl.BlockSpec(memory_space=pltpu.SMEM)
    vmem = pl.BlockSpec(memory_space=pltpu.VMEM)
    outs = [out] if single else list(out)
    got = pl.pallas_call(
        kernel,
        in_specs=[smem] * scalars + [vmem] * (len(args) - scalars),
        out_specs=[vmem] * len(outs),
        out_shape=outs,
        scratch_shapes=scratch,
        cost_estimate=cost,
        compiler_params=PARAMS,
    )(*args)
    return got[0] if single else got


def like(*shape, dtype=BF):
    return jax.ShapeDtypeStruct(shape, dtype)


def others(x, axis):
    n = lax.axis_size(axis)
    sent = {k: lax.ppermute(x, axis, [(i, i ^ k) for i in range(n)]) for k in (1, 3, 2)}
    return [sent[k] for k in (1, 2, 3)]


def per_device(acts, grads, basis_in, basis_out, lengths):
    zhi, core, y, zh, zq = (lax.axis_index(a) for a in ("zhi", "core", "y", "zh", "zq"))
    crossed = (core != zhi).astype(jnp.int32)
    tokens = (y >> 1) ^ zhi
    where = jnp.stack([zh, crossed, lengths[0, 0], core, zq, y, (y & 1) ^ tokens, tokens])
    lines, partial = pl.pallas_call(
        start_kernel,
        in_specs=[pl.BlockSpec(memory_space=pltpu.SMEM)] + [pl.BlockSpec(memory_space=pl.ANY)] * 3,
        out_specs=[pl.BlockSpec(memory_space=pltpu.VMEM)] * 2,
        out_shape=[like(VALID, WIDE), like(4, VALID, WIDE)],
        scratch_shapes=[pltpu.VMEM(x.shape, BF) for x in (acts, basis_in, grads)]
        + [pltpu.SemaphoreType.DMA] * 3,
        compiler_params=pltpu.CompilerParams(vmem_limit_bytes=60 << 20),
    )(lengths, grads, acts, basis_in)
    near = lax.ppermute(lines, PLANE, to_basis(False))
    far = lax.ppermute(lines, PLANE, to_basis(True))
    partial = exchange(partial, "y")
    basis = basis_out[0].T
    cols = basis.shape[0]
    other_basis = swap(basis, "core")
    both = call(join_kernel, like(4, 2, VALID, WIDE), near, far, partial, scalars=0)
    both = exchange(both, "zq")
    lines = call(sort_kernel, like(VALID, 8 * FEAT), where, both)
    ins = call(pack_kernel, like(16, 80, 128), where, both)
    lines = [lines] + others(lines, "y")
    ins = exchange(ins, ("zhi", "zh", "zq"))
    part = project(where, lines, basis, other_basis)
    part, ins = lax.optimization_barrier((part, ins))
    ins = call(merge_kernel, like(2, VALID + 8, WIDE), ins, scalars=0)
    part = exchange(part, "x")
    part = call(sum_kernel, like(72, cols), part, scalars=0)
    part, ins = lax.optimization_barrier((part, ins))
    ins = [ins] + others(ins, "y")
    part = call(spread_kernel, like(4, 72, cols), part, swap(part, "zhi"), scalars=0, cost=HINT)
    ins = jnp.stack(ins)
    other_ins = swap(ins, "core")
    outs = exchange(part, "x").reshape(2, VALID, cols)
    ins, masks = call(
        arrange_kernel,
        [like(4, VALID, 1024), like(4, 8, VALID)],
        where,
        ins,
        other_ins,
    )
    left = call(left_kernel, like(2, cols, VALID), outs, scalars=0, cost=HINT)
    return squares(where, left, swap(outs, "core"), ins, masks)


def solution(mesh):
    axes = ("zhi", "core", "x", "y", "zh", "zq")
    fine = Mesh(mesh.devices.reshape(2, 2, 4, 4, 2, 4), axes)
    grp, row, col = ("zhi", "core"), "x", ("y", "zh", "zq")
    in_specs = (
        P(grp, col),
        P(grp, (row, *col)),
        P(col, row),
        P(row, grp, col),
        P(grp, None),
    )
    return jax.shard_map(
        per_device, mesh=fine, in_specs=in_specs, out_specs=P(col, row), check_vma=False
    )
```

```python
import jax
import jax.numpy as jnp
from jax import lax
from jax.experimental import pallas as pl
from jax.experimental.pallas import tpu as pltpu
from jax.sharding import Mesh, PartitionSpec as P

LEN = 96
VALID = 144
FEAT = 224
WIDE = 256
BF = jnp.bfloat16
F32 = jnp.float32
HINT = pl.CostEstimate(flops=int(5e9), bytes_accessed=int(1e6), transcendentals=0)
LONG = pl.CostEstimate(flops=int(8e9), bytes_accessed=int(1e6), transcendentals=0)
PLANE = ("zhi", "core", "y", "zh", "zq")
PARAMS = pltpu.CompilerParams(vmem_limit_bytes=16 << 20)


def to_basis(far):
    def place(zhi, core, y, zlo):
        return ((zhi * 2 + core) * 4 + y) * 8 + zlo

    pairs = []
    for zhi in range(2):
        for core in range(2):
            for y in range(4):
                for z in range(8):
                    crossed = zhi != y >> 1
                    to = (z ^ 3 if far else z ^ 4) if crossed else (z ^ 4 if far else z)
                    to_y = 2 * (core ^ (y >> 1)) + ((y & 1) ^ core)
                    there = place(y >> 1, zhi, to_y, to)
                    pairs.append((place(zhi, core, y, z), there))
    return pairs


def exchange(x, axis):
    return lax.all_to_all(x, axis, 0, 0, tiled=True)


def everywhere(x, axis):
    return exchange(jnp.broadcast_to(x[None], (lax.axis_size(axis),) + x.shape), axis)


def swap(x, axis):
    return lax.ppermute(x, axis, [(0, 1), (1, 0)])


def across(left, right):
    return lax.dot_general(left, right, (((1,), (1,)), ((), ())), preferred_element_type=F32)


def chosen(first):
    slot = lax.broadcasted_iota(jnp.int32, (VALID, 2 * LEN), 0)
    line = lax.broadcasted_iota(jnp.int32, (VALID, 2 * LEN), 1)
    source = jnp.where(slot < first, slot, slot - first + LEN)
    return (source == line).astype(F32).astype(BF)


def start_kernel(len_ref, grads_hbm, acts_hbm, basis_hbm, lines_ref, part_ref, *scratch):
    held, sems = scratch[:3], scratch[3:]
    copies = [
        pltpu.make_async_copy(source, ref, sem)
        for source, ref, sem in zip((acts_hbm, basis_hbm, grads_hbm), held, sems)
    ]
    for copy in copies:
        copy.start()
    acts_ref, basis_ref, grads_ref = held
    pick = chosen(len_ref[0, 0])
    copies[0].wait()
    lines = jnp.dot(pick, acts_ref[...], preferred_element_type=F32).astype(BF)
    copies[1].wait()
    for y in range(4):
        part_ref[y] = jnp.dot(
            lines, basis_ref[:, y * WIDE : (y + 1) * WIDE], preferred_element_type=F32
        ).astype(BF)
    copies[2].wait()
    lines_ref[:, :FEAT] = jnp.dot(pick, grads_ref[...], preferred_element_type=F32).astype(BF)
    lines_ref[:, FEAT:] = jnp.zeros((VALID, WIDE - FEAT), BF)


def join_kernel(near_ref, far_ref, parts_ref, out_ref):
    total = parts_ref[0].astype(F32)
    for y in range(1, 4):
        total += parts_ref[y].astype(F32)
    total = total.astype(BF)
    for d in range(4):
        for w, ref in enumerate((near_ref, far_ref)):
            at = d * 64 + w * 32
            out_ref[d, w] = jnp.concatenate([ref[:, :FEAT], total[:, at : at + 32]], axis=1)


def sort_kernel(where_ref, both_ref, out_ref, half_ref):
    zh, crossed = where_ref[0], where_ref[1]
    for f in range(8):
        far = (jnp.int32(f // 4) != zh).astype(jnp.int32) ^ crossed
        at = (f % 4) ^ (3 * (far & crossed))
        out_ref[:, f * FEAT : (f + 1) * FEAT] = both_ref[at, far][:, :FEAT]
    half = VALID // 2
    half_ref[...] = jnp.where(where_ref[4] % 2 == 0, out_ref[:half], out_ref[half:])


def pack_kernel(where_ref, both_ref, in_ref):
    sums = []
    for w in range(2):
        total = both_ref[0, w][:, FEAT:].astype(F32)
        for q in range(1, 4):
            total += both_ref[q, w][:, FEAT:].astype(F32)
        sums.append(total)
    half = VALID // 2
    packed = jnp.concatenate([x[i : i + half] for i in (0, half) for x in sums], axis=1)
    count = jnp.full((8, 128), where_ref[2], jnp.int32).astype(F32).astype(BF)
    for copy in range(16):
        in_ref[copy, :half] = packed.astype(BF)
        in_ref[copy, half:] = count


def merge_kernel(parts_ref, out_ref):
    half = VALID // 2
    for zhi in range(2):
        for q in range(4):
            at = zhi * 8 + q
            total = parts_ref[at, :half].astype(F32) + parts_ref[at + 4, :half].astype(F32)
            total = total.astype(BF)
            out_ref[zhi, :half, q * 64 : q * 64 + 64] = total[:, :64]
            out_ref[zhi, half:VALID, q * 64 : q * 64 + 64] = total[:, 64:]
        for h in range(2):
            out_ref[zhi, VALID:, h * 128 : h * 128 + 128] = parts_ref[zhi * 8, half:]


def project_kernel(
    where_ref, a_ref, b_ref, c_ref, e_ref, d_ref, own_ref, other_ref, out_ref, held, total_ref
):
    step = pl.program_id(0)
    tokens, same = where_ref[7], where_ref[3] == where_ref[6]
    even = where_ref[4] % 2 == 0
    mine, next_ = c_ref[...], e_ref[...]
    far = jnp.concatenate([jnp.where(even, mine, next_), jnp.where(even, next_, mine)], axis=0)
    for left, right, t in (
        (a_ref[...], b_ref[...], tokens),
        (d_ref[...], far, 1 - tokens),
    ):
        held[0, t] = jnp.where(same, left, right)
        held[1, t] = jnp.where(same, right, left)
    rows = (2 * VALID, held.shape[3])
    total = across(held[0].reshape(rows), own_ref[...])
    total += across(held[1].reshape(rows), other_ref[...])

    @pl.when(step == 0)
    def _():
        total_ref[...] = total

    @pl.when(step > 0)
    def _():
        total_ref[...] += total

    @pl.when(step == pl.num_programs(0) - 1)
    def _():
        for h in range(4):
            out_ref[h] = total_ref[h * 72 : (h + 1) * 72].astype(BF)


def project(where, lines, basis, other_basis):
    cols, rows = basis.shape
    deep = rows // 2
    line = [pl.BlockSpec((x.shape[0], deep), lambda k: (0, k)) for x in lines]
    rotated = pl.BlockSpec((cols, deep), lambda k: (0, k))
    return pl.pallas_call(
        project_kernel,
        grid=(rows // deep,),
        in_specs=[pl.BlockSpec(memory_space=pltpu.SMEM)] + line + [rotated] * 2,
        out_specs=pl.BlockSpec((4, 72, cols), lambda k: (0, 0, 0)),
        out_shape=like(4, 72, cols),
        scratch_shapes=[pltpu.VMEM((2, 2, VALID, deep), BF), pltpu.VMEM((2 * VALID, cols), F32)],
        compiler_params=PARAMS,
        cost_estimate=LONG,
    )(where, *lines, basis, other_basis)


def sum_kernel(parts_ref, out_ref):
    total = parts_ref[0].astype(F32)
    for x in range(1, 4):
        total += parts_ref[x].astype(F32)
    out_ref[...] = total.astype(BF)


def spread_kernel(one_ref, two_ref, out_ref):
    total = (one_ref[...].astype(F32) + two_ref[...].astype(F32)).astype(BF)
    for x in range(4):
        out_ref[x] = total


def arrange_kernel(where_ref, own_ref, other_ref, out_ref, mask_ref):
    core = where_ref[3]
    slot = lax.broadcasted_iota(jnp.int32, (8, VALID), 1).astype(F32)
    for zhi in range(2):
        for c in range(2):
            mine = core == c
            g = zhi * 2 + c
            for y in range(4):
                k = y ^ where_ref[5]
                block = jnp.where(mine, own_ref[k, zhi], other_ref[k, zhi])
                out_ref[g, :, y * WIDE : (y + 1) * WIDE] = block[:VALID]
            count = block[VALID:, :VALID].astype(F32)
            mask_ref[g] = (slot < count).astype(F32).astype(BF)


def left_kernel(lines_ref, left_ref):
    for t in range(2):
        left_ref[t] = lines_ref[t].T


def square_kernel(where_ref, own_ref, other_ref, in_ref, mask_ref, eig_ref, left_ref):
    core = where_ref[3]

    @pl.when(pl.program_id(0) == 0)
    def _():
        for t in range(2):
            for at, lines in (
                (2 * core + t, own_ref[t]),
                (2 * (1 - core) + t, other_ref[t].T),
            ):
                first = lines * mask_ref[at][:1]
                left_ref[2 * at] = first
                left_ref[2 * at + 1] = lines - first

    rows = 224
    for o in range(448 // rows):
        total = jnp.zeros((rows, eig_ref.shape[1]), F32)
        for s in range(8):
            block = jnp.dot(
                left_ref[s, o * rows : (o + 1) * rows, :],
                in_ref[s // 2],
                preferred_element_type=F32,
            )
            total += block * block
        eig_ref[o * rows : (o + 1) * rows] = total * (1.0 / 768.0)


def squares(where, left, other, ins, masks):
    cols, wide, tile = left.shape[1], ins.shape[2], 256
    whole = lambda x: pl.BlockSpec(x.shape, lambda i: (0, 0, 0))
    return pl.pallas_call(
        square_kernel,
        grid=(wide // tile,),
        in_specs=[
            pl.BlockSpec(memory_space=pltpu.SMEM),
            whole(left),
            whole(other),
            pl.BlockSpec((4, VALID, tile), lambda i: (0, 0, i)),
            whole(masks),
        ],
        out_specs=pl.BlockSpec((cols, tile), lambda i: (0, i)),
        out_shape=like(cols, wide, dtype=F32),
        scratch_shapes=[pltpu.VMEM((8, cols, VALID), BF)],
        compiler_params=PARAMS,
    )(where, left, other, ins, masks)


def call(kernel, out, *args, scalars=1, scratch=(), cost=None):
    single = not isinstance(out, (list, tuple))
    smem = pl.BlockSpec(memory_space=pltpu.SMEM)
    vmem = pl.BlockSpec(memory_space=pltpu.VMEM)
    outs = [out] if single else list(out)
    got = pl.pallas_call(
        kernel,
        in_specs=[smem] * scalars + [vmem] * (len(args) - scalars),
        out_specs=[vmem] * len(outs),
        out_shape=outs,
        scratch_shapes=scratch,
        cost_estimate=cost,
        compiler_params=PARAMS,
    )(*args)
    return got[0] if single else got


def like(*shape, dtype=BF):
    return jax.ShapeDtypeStruct(shape, dtype)


def others(x, axis):
    n = lax.axis_size(axis)
    sent = {k: lax.ppermute(x, axis, [(i, i ^ k) for i in range(n)]) for k in (1, 3, 2)}
    return [sent[k] for k in (1, 2, 3)]


def per_device(acts, grads, basis_in, basis_out, lengths):
    zhi, core, y, zh, zq = (lax.axis_index(a) for a in ("zhi", "core", "y", "zh", "zq"))
    crossed = (core != zhi).astype(jnp.int32)
    tokens = (y >> 1) ^ zhi
    where = jnp.stack([zh, crossed, lengths[0, 0], core, zq, y, (y & 1) ^ tokens, tokens])
    lines, partial = pl.pallas_call(
        start_kernel,
        in_specs=[pl.BlockSpec(memory_space=pltpu.SMEM)] + [pl.BlockSpec(memory_space=pl.ANY)] * 3,
        out_specs=[pl.BlockSpec(memory_space=pltpu.VMEM)] * 2,
        out_shape=[like(VALID, WIDE), like(4, VALID, WIDE)],
        scratch_shapes=[pltpu.VMEM(x.shape, BF) for x in (acts, basis_in, grads)]
        + [pltpu.SemaphoreType.DMA] * 3,
        compiler_params=pltpu.CompilerParams(vmem_limit_bytes=60 << 20),
    )(lengths, grads, acts, basis_in)
    near = lax.ppermute(lines, PLANE, to_basis(False))
    far = lax.ppermute(lines, PLANE, to_basis(True))
    partial = exchange(partial, "y")
    basis = basis_out[0].T
    cols = basis.shape[0]
    other_basis = swap(basis, "core")
    both = call(join_kernel, like(4, 2, VALID, WIDE), near, far, partial, scalars=0)
    both = exchange(both, "zq")
    lines, half = call(
        sort_kernel, [like(VALID, 8 * FEAT), like(VALID // 2, 8 * FEAT)], where, both
    )
    ins = call(pack_kernel, like(16, 80, 128), where, both)
    two = lax.ppermute(half, "y", [(i, i ^ 2) for i in range(4)])
    one, three = (lax.ppermute(lines, "y", [(i, i ^ k) for i in range(4)]) for k in (1, 3))
    lines = [lines, one, two, lax.ppermute(two, "zq", [(i, i ^ 1) for i in range(4)]), three]
    ins = exchange(ins, ("zhi", "zh", "zq"))
    part = project(where, lines, basis, other_basis)
    part, ins = lax.optimization_barrier((part, ins))
    ins = call(merge_kernel, like(2, VALID + 8, WIDE), ins, scalars=0)
    part = exchange(part, "x")
    part = call(sum_kernel, like(72, cols), part, scalars=0)
    part, ins = lax.optimization_barrier((part, ins))
    ins = [ins] + others(ins, "y")
    part = call(spread_kernel, like(4, 72, cols), part, swap(part, "zhi"), scalars=0, cost=HINT)
    ins = jnp.stack(ins)
    other_ins = swap(ins, "core")
    outs = exchange(part, "x").reshape(2, VALID, cols)
    ins, masks = call(
        arrange_kernel,
        [like(4, VALID, 1024), like(4, 8, VALID)],
        where,
        ins,
        other_ins,
    )
    left = call(left_kernel, like(2, cols, VALID), outs, scalars=0, cost=HINT)
    return squares(where, left, swap(outs, "core"), ins, masks)


def solution(mesh):
    axes = ("zhi", "core", "x", "y", "zh", "zq")
    fine = Mesh(mesh.devices.reshape(2, 2, 4, 4, 2, 4), axes)
    grp, row, col = ("zhi", "core"), "x", ("y", "zh", "zq")
    in_specs = (
        P(grp, col),
        P(grp, (row, *col)),
        P(col, row),
        P(row, grp, col),
        P(grp, None),
    )
    return jax.shard_map(
        per_device, mesh=fine, in_specs=in_specs, out_specs=P(col, row), check_vma=False
    )
```

```python
import jax
import jax.numpy as jnp
from jax import lax
from jax.experimental import pallas as pl
from jax.experimental.pallas import tpu as pltpu
from jax.sharding import Mesh, PartitionSpec as P

LEN = 96
VALID = 144
FEAT = 224
WIDE = 256
BF = jnp.bfloat16
F32 = jnp.float32
HINT = pl.CostEstimate(flops=int(5e9), bytes_accessed=int(1e6), transcendentals=0)
LONG = pl.CostEstimate(flops=int(3e10), bytes_accessed=int(1e6), transcendentals=0)
PLANE = ("zhi", "core", "y", "zh", "zq")
PARAMS = pltpu.CompilerParams(vmem_limit_bytes=16 << 20)


def to_basis(far):
    def place(zhi, core, y, zlo):
        return ((zhi * 2 + core) * 4 + y) * 8 + zlo

    pairs = []
    for zhi in range(2):
        for core in range(2):
            for y in range(4):
                for z in range(8):
                    crossed = zhi != y >> 1
                    to = (z ^ 3 if far else z ^ 4) if crossed else (z ^ 4 if far else z)
                    to_y = 2 * (core ^ (y >> 1)) + ((y & 1) ^ core)
                    there = place(y >> 1, zhi, to_y, to)
                    pairs.append((place(zhi, core, y, z), there))
    return pairs


def exchange(x, axis):
    return lax.all_to_all(x, axis, 0, 0, tiled=True)


def everywhere(x, axis):
    return exchange(jnp.broadcast_to(x[None], (lax.axis_size(axis),) + x.shape), axis)


def swap(x, axis):
    return lax.ppermute(x, axis, [(0, 1), (1, 0)])


def across(left, right):
    return lax.dot_general(left, right, (((1,), (1,)), ((), ())), preferred_element_type=F32)


def chosen(first):
    slot = lax.broadcasted_iota(jnp.int32, (VALID, 2 * LEN), 0)
    line = lax.broadcasted_iota(jnp.int32, (VALID, 2 * LEN), 1)
    source = jnp.where(slot < first, slot, slot - first + LEN)
    return (source == line).astype(F32).astype(BF)


def start_kernel(len_ref, grads_hbm, acts_hbm, basis_hbm, lines_ref, part_ref, *scratch):
    held, sems = scratch[:3], scratch[3:]
    copies = [
        pltpu.make_async_copy(source, ref, sem)
        for source, ref, sem in zip((acts_hbm, basis_hbm, grads_hbm), held, sems)
    ]
    for copy in copies:
        copy.start()
    acts_ref, basis_ref, grads_ref = held
    pick = chosen(len_ref[0, 0])
    copies[0].wait()
    lines = jnp.dot(pick, acts_ref[...], preferred_element_type=F32).astype(BF)
    copies[1].wait()
    for y in range(4):
        part_ref[y] = jnp.dot(
            lines, basis_ref[:, y * WIDE : (y + 1) * WIDE], preferred_element_type=F32
        ).astype(BF)
    copies[2].wait()
    lines_ref[:, :FEAT] = jnp.dot(pick, grads_ref[...], preferred_element_type=F32).astype(BF)
    lines_ref[:, FEAT:] = jnp.zeros((VALID, WIDE - FEAT), BF)


def pair_kernel(near_ref, far_ref, out_ref):
    out_ref[0] = near_ref[...]
    out_ref[1] = far_ref[...]


def join_kernel(pair_ref, parts_ref, out_ref):
    total = parts_ref[0].astype(F32)
    for y in range(1, 4):
        total += parts_ref[y].astype(F32)
    total = total.astype(BF)
    for d in range(4):
        for w in range(2):
            at = d * 64 + w * 32
            out_ref[d, w] = jnp.concatenate(
                [pair_ref[w][:, :FEAT], total[:, at : at + 32]], axis=1
            )


def sort_kernel(where_ref, both_ref, out_ref):
    zh, crossed = where_ref[0], where_ref[1]
    for f in range(8):
        far = (jnp.int32(f // 4) != zh).astype(jnp.int32) ^ crossed
        at = (f % 4) ^ (3 * (far & crossed))
        out_ref[:, f * FEAT : (f + 1) * FEAT] = both_ref[at, far][:, :FEAT]


def pack_kernel(where_ref, both_ref, in_ref):
    sums = []
    for w in range(2):
        total = both_ref[0, w][:, FEAT:].astype(F32)
        for q in range(1, 4):
            total += both_ref[q, w][:, FEAT:].astype(F32)
        sums.append(total)
    half = VALID // 2
    packed = jnp.concatenate([x[i : i + half] for i in (0, half) for x in sums], axis=1)
    count = jnp.full((8, 128), where_ref[2], jnp.int32).astype(F32).astype(BF)
    for copy in range(16):
        in_ref[copy, :half] = packed.astype(BF)
        in_ref[copy, half:] = count


def merge_kernel(parts_ref, out_ref):
    half = VALID // 2
    for zhi in range(2):
        for q in range(4):
            at = zhi * 8 + q
            total = parts_ref[at, :half].astype(F32) + parts_ref[at + 4, :half].astype(F32)
            total = total.astype(BF)
            out_ref[zhi, :half, q * 64 : q * 64 + 64] = total[:, :64]
            out_ref[zhi, half:VALID, q * 64 : q * 64 + 64] = total[:, 64:]
        for h in range(2):
            out_ref[zhi, VALID:, h * 128 : h * 128 + 128] = parts_ref[zhi * 8, half:]


def project_kernel(
    where_ref, a_ref, b_ref, c_ref, d_ref, own_ref, other_ref, out_ref, held, total_ref
):
    step = pl.program_id(0)
    tokens, same = where_ref[7], where_ref[3] == where_ref[6]
    for left_ref, right_ref, t in ((a_ref, b_ref, tokens), (d_ref, c_ref, 1 - tokens)):
        left, right = left_ref[...], right_ref[...]
        held[0, t] = jnp.where(same, left, right)
        held[1, t] = jnp.where(same, right, left)
    rows = (2 * VALID, held.shape[3])
    total = across(held[0].reshape(rows), own_ref[...])
    total += across(held[1].reshape(rows), other_ref[...])

    @pl.when(step == 0)
    def _():
        total_ref[...] = total

    @pl.when(step > 0)
    def _():
        total_ref[...] += total

    @pl.when(step == pl.num_programs(0) - 1)
    def _():
        for h in range(4):
            out_ref[h] = total_ref[h * 72 : (h + 1) * 72].astype(BF)


def project(where, lines, basis, other_basis):
    cols, rows = basis.shape
    deep = rows // 2
    line = pl.BlockSpec((VALID, deep), lambda k: (0, k))
    rotated = pl.BlockSpec((cols, deep), lambda k: (0, k))
    return pl.pallas_call(
        project_kernel,
        grid=(rows // deep,),
        in_specs=[pl.BlockSpec(memory_space=pltpu.SMEM)] + [line] * 4 + [rotated] * 2,
        out_specs=pl.BlockSpec((4, 72, cols), lambda k: (0, 0, 0)),
        out_shape=like(4, 72, cols),
        scratch_shapes=[pltpu.VMEM((2, 2, VALID, deep), BF), pltpu.VMEM((2 * VALID, cols), F32)],
        compiler_params=PARAMS,
        cost_estimate=LONG,
    )(where, *lines, basis, other_basis)


def sum_kernel(parts_ref, out_ref):
    total = parts_ref[0].astype(F32)
    for x in range(1, 4):
        total += parts_ref[x].astype(F32)
    out_ref[...] = total.astype(BF)


def spread_kernel(one_ref, two_ref, out_ref):
    total = (one_ref[...].astype(F32) + two_ref[...].astype(F32)).astype(BF)
    for x in range(4):
        out_ref[x] = total


def arrange_kernel(where_ref, own_ref, other_ref, out_ref, mask_ref):
    core = where_ref[3]
    slot = lax.broadcasted_iota(jnp.int32, (8, VALID), 1).astype(F32)
    for zhi in range(2):
        for c in range(2):
            mine = core == c
            g = zhi * 2 + c
            for y in range(4):
                k = y ^ where_ref[5]
                block = jnp.where(mine, own_ref[k, zhi], other_ref[k, zhi])
                out_ref[g, :, y * WIDE : (y + 1) * WIDE] = block[:VALID]
            count = block[VALID:, :VALID].astype(F32)
            mask_ref[g] = (slot < count).astype(F32).astype(BF)


def left_kernel(lines_ref, left_ref):
    for t in range(2):
        left_ref[t] = lines_ref[t].T


def square_kernel(where_ref, own_ref, other_ref, in_ref, mask_ref, eig_ref, left_ref):
    core = where_ref[3]

    @pl.when(pl.program_id(0) == 0)
    def _():
        for t in range(2):
            for at, lines in (
                (2 * core + t, own_ref[t]),
                (2 * (1 - core) + t, other_ref[t].T),
            ):
                first = lines * mask_ref[at][:1]
                left_ref[2 * at] = first
                left_ref[2 * at + 1] = lines - first

    rows = 224
    for o in range(448 // rows):
        total = jnp.zeros((rows, eig_ref.shape[1]), F32)
        for s in range(8):
            block = jnp.dot(
                left_ref[s, o * rows : (o + 1) * rows, :],
                in_ref[s // 2],
                preferred_element_type=F32,
            )
            total += block * block
        eig_ref[o * rows : (o + 1) * rows] = total / 768.0


def squares(where, left, other, ins, masks):
    cols, wide, tile = left.shape[1], ins.shape[2], 256
    whole = lambda x: pl.BlockSpec(x.shape, lambda i: (0, 0, 0))
    return pl.pallas_call(
        square_kernel,
        grid=(wide // tile,),
        in_specs=[
            pl.BlockSpec(memory_space=pltpu.SMEM),
            whole(left),
            whole(other),
            pl.BlockSpec((4, VALID, tile), lambda i: (0, 0, i)),
            whole(masks),
        ],
        out_specs=pl.BlockSpec((cols, tile), lambda i: (0, i)),
        out_shape=like(cols, wide, dtype=F32),
        scratch_shapes=[pltpu.VMEM((8, cols, VALID), BF)],
        compiler_params=PARAMS,
    )(where, left, other, ins, masks)


def call(kernel, out, *args, scalars=1, scratch=(), cost=None):
    single = not isinstance(out, (list, tuple))
    smem = pl.BlockSpec(memory_space=pltpu.SMEM)
    vmem = pl.BlockSpec(memory_space=pltpu.VMEM)
    outs = [out] if single else list(out)
    got = pl.pallas_call(
        kernel,
        in_specs=[smem] * scalars + [vmem] * (len(args) - scalars),
        out_specs=[vmem] * len(outs),
        out_shape=outs,
        scratch_shapes=scratch,
        cost_estimate=cost,
        compiler_params=PARAMS,
    )(*args)
    return got[0] if single else got


def like(*shape, dtype=BF):
    return jax.ShapeDtypeStruct(shape, dtype)


def others(x, axis):
    n = lax.axis_size(axis)
    sent = {k: lax.ppermute(x, axis, [(i, i ^ k) for i in range(n)]) for k in (1, 3, 2)}
    return [sent[k] for k in (1, 2, 3)]


def per_device(acts, grads, basis_in, basis_out, lengths):
    zhi, core, y, zh, zq = (lax.axis_index(a) for a in ("zhi", "core", "y", "zh", "zq"))
    crossed = (core != zhi).astype(jnp.int32)
    tokens = (y >> 1) ^ zhi
    where = jnp.stack([zh, crossed, lengths[0, 0], core, zq, y, (y & 1) ^ tokens, tokens])
    lines, partial = pl.pallas_call(
        start_kernel,
        in_specs=[pl.BlockSpec(memory_space=pltpu.SMEM)] + [pl.BlockSpec(memory_space=pl.ANY)] * 3,
        out_specs=[pl.BlockSpec(memory_space=pltpu.VMEM)] * 2,
        out_shape=[like(VALID, WIDE), like(4, VALID, WIDE)],
        scratch_shapes=[pltpu.VMEM(x.shape, BF) for x in (acts, basis_in, grads)]
        + [pltpu.SemaphoreType.DMA] * 3,
        compiler_params=pltpu.CompilerParams(vmem_limit_bytes=60 << 20),
    )(lengths, grads, acts, basis_in)
    near = lax.ppermute(lines, PLANE, to_basis(False))
    far = lax.ppermute(lines, PLANE, to_basis(True))
    partial = exchange(partial, "y")
    basis = basis_out[0].T
    cols = basis.shape[0]
    other_basis = swap(basis, "core")
    both = call(pair_kernel, like(2, VALID, WIDE), near, far, scalars=0, cost=HINT)
    both = call(join_kernel, like(4, 2, VALID, WIDE), both, partial, scalars=0)
    both = exchange(both, "zq")
    lines = call(sort_kernel, like(VALID, 8 * FEAT), where, both)
    ins = call(pack_kernel, like(16, 80, 128), where, both)
    lines = [lines] + others(lines, "y")
    ins = exchange(ins, ("zhi", "zh", "zq"))
    part = project(where, lines, basis, other_basis)
    part, ins = lax.optimization_barrier((part, ins))
    ins = call(merge_kernel, like(2, VALID + 8, WIDE), ins, scalars=0)
    part = exchange(part, "x")
    part = call(sum_kernel, like(72, cols), part, scalars=0)
    part, ins = lax.optimization_barrier((part, ins))
    ins = [ins] + others(ins, "y")
    part = call(spread_kernel, like(4, 72, cols), part, swap(part, "zhi"), scalars=0, cost=HINT)
    ins = jnp.stack(ins)
    other_ins = swap(ins, "core")
    outs = exchange(part, "x").reshape(2, VALID, cols)
    ins, masks = call(
        arrange_kernel,
        [like(4, VALID, 1024), like(4, 8, VALID)],
        where,
        ins,
        other_ins,
    )
    left = call(left_kernel, like(2, cols, VALID), outs, scalars=0, cost=HINT)
    return squares(where, left, swap(outs, "core"), ins, masks)


def solution(mesh):
    axes = ("zhi", "core", "x", "y", "zh", "zq")
    fine = Mesh(mesh.devices.reshape(2, 2, 4, 4, 2, 4), axes)
    grp, row, col = ("zhi", "core"), "x", ("y", "zh", "zq")
    in_specs = (
        P(grp, col),
        P(grp, (row, *col)),
        P(col, row),
        P(row, grp, col),
        P(grp, None),
    )
    return jax.shard_map(
        per_device, mesh=fine, in_specs=in_specs, out_specs=P(col, row), check_vma=False
    )
```

```python
import jax
import jax.numpy as jnp
from jax import lax
from jax.experimental import pallas as pl
from jax.experimental.pallas import tpu as pltpu
from jax.sharding import Mesh, PartitionSpec as P

LEN = 96
VALID = 144
FEAT = 224
WIDE = 256
BF = jnp.bfloat16
F32 = jnp.float32
HINT = pl.CostEstimate(flops=int(5e9), bytes_accessed=int(1e6), transcendentals=0)
LONG = pl.CostEstimate(flops=int(3e10), bytes_accessed=int(1e6), transcendentals=0)
PLANE = ("zhi", "core", "y", "zh", "zq")
PARAMS = pltpu.CompilerParams(vmem_limit_bytes=16 << 20)


def to_basis(far):
    def place(zhi, core, y, zlo):
        return ((zhi * 2 + core) * 4 + y) * 8 + zlo

    pairs = []
    for zhi in range(2):
        for core in range(2):
            for y in range(4):
                for z in range(8):
                    crossed = zhi != y >> 1
                    to = (z ^ 3 if far else z ^ 4) if crossed else (z ^ 4 if far else z)
                    to_y = 2 * (core ^ (y >> 1)) + ((y & 1) ^ core)
                    there = place(y >> 1, zhi, to_y, to)
                    pairs.append((place(zhi, core, y, z), there))
    return pairs


def exchange(x, axis):
    return lax.all_to_all(x, axis, 0, 0, tiled=True)


def everywhere(x, axis):
    return exchange(jnp.broadcast_to(x[None], (lax.axis_size(axis),) + x.shape), axis)


def swap(x, axis):
    return lax.ppermute(x, axis, [(0, 1), (1, 0)])


def across(left, right):
    return lax.dot_general(left, right, (((1,), (1,)), ((), ())), preferred_element_type=F32)


def chosen(first):
    slot = lax.broadcasted_iota(jnp.int32, (VALID, 2 * LEN), 0)
    line = lax.broadcasted_iota(jnp.int32, (VALID, 2 * LEN), 1)
    source = jnp.where(slot < first, slot, slot - first + LEN)
    return (source == line).astype(F32).astype(BF)


def start_kernel(len_ref, grads_hbm, acts_hbm, basis_hbm, lines_ref, part_ref, *scratch):
    held, sems = scratch[:3], scratch[3:]
    copies = [
        pltpu.make_async_copy(source, ref, sem)
        for source, ref, sem in zip((acts_hbm, basis_hbm, grads_hbm), held, sems)
    ]
    for copy in copies:
        copy.start()
    acts_ref, basis_ref, grads_ref = held
    pick = chosen(len_ref[0, 0])
    copies[0].wait()
    lines = jnp.dot(pick, acts_ref[...], preferred_element_type=F32).astype(BF)
    copies[1].wait()
    for y in range(4):
        part_ref[y] = jnp.dot(
            lines, basis_ref[:, y * WIDE : (y + 1) * WIDE], preferred_element_type=F32
        ).astype(BF)
    copies[2].wait()
    lines_ref[:, :FEAT] = jnp.dot(pick, grads_ref[...], preferred_element_type=F32).astype(BF)
    lines_ref[:, FEAT:] = jnp.zeros((VALID, WIDE - FEAT), BF)


def pair_kernel(near_ref, far_ref, out_ref):
    out_ref[0] = near_ref[...]
    out_ref[1] = far_ref[...]


def join_kernel(pair_ref, parts_ref, out_ref):
    total = parts_ref[0].astype(F32)
    for y in range(1, 4):
        total += parts_ref[y].astype(F32)
    total = total.astype(BF)
    for d in range(4):
        for w in range(2):
            at = d * 64 + w * 32
            out_ref[d, w] = jnp.concatenate(
                [pair_ref[w][:, :FEAT], total[:, at : at + 32]], axis=1
            )


def sort_kernel(where_ref, both_ref, out_ref, in_ref):
    zh, crossed = where_ref[0], where_ref[1]
    for f in range(8):
        far = (jnp.int32(f // 4) != zh).astype(jnp.int32) ^ crossed
        at = (f % 4) ^ (3 * (far & crossed))
        out_ref[:, f * FEAT : (f + 1) * FEAT] = both_ref[at, far][:, :FEAT]
    sums = []
    for w in range(2):
        total = both_ref[0, w][:, FEAT:].astype(F32)
        for q in range(1, 4):
            total += both_ref[q, w][:, FEAT:].astype(F32)
        sums.append(total)
    half = VALID // 2
    packed = jnp.concatenate([x[i : i + half] for i in (0, half) for x in sums], axis=1)
    count = jnp.full((8, 128), where_ref[2], jnp.int32).astype(F32).astype(BF)
    for copy in range(16):
        in_ref[copy, :half] = packed.astype(BF)
        in_ref[copy, half:] = count


def merge_kernel(parts_ref, out_ref):
    half = VALID // 2
    for zhi in range(2):
        for q in range(4):
            at = zhi * 8 + q
            total = parts_ref[at, :half].astype(F32) + parts_ref[at + 4, :half].astype(F32)
            total = total.astype(BF)
            out_ref[zhi, :half, q * 64 : q * 64 + 64] = total[:, :64]
            out_ref[zhi, half:VALID, q * 64 : q * 64 + 64] = total[:, 64:]
        for h in range(2):
            out_ref[zhi, VALID:, h * 128 : h * 128 + 128] = parts_ref[zhi * 8, half:]


def project_kernel(
    where_ref, a_ref, b_ref, c_ref, d_ref, own_ref, other_ref, out_ref, held, total_ref
):
    step = pl.program_id(0)
    tokens, same = where_ref[7], where_ref[3] == where_ref[6]
    for left_ref, right_ref, t in ((a_ref, b_ref, tokens), (d_ref, c_ref, 1 - tokens)):
        left, right = left_ref[...], right_ref[...]
        held[0, t] = jnp.where(same, left, right)
        held[1, t] = jnp.where(same, right, left)
    rows = (2 * VALID, held.shape[3])
    total = across(held[0].reshape(rows), own_ref[...])
    total += across(held[1].reshape(rows), other_ref[...])

    @pl.when(step == 0)
    def _():
        total_ref[...] = total

    @pl.when(step > 0)
    def _():
        total_ref[...] += total

    @pl.when(step == pl.num_programs(0) - 1)
    def _():
        for h in range(4):
            out_ref[h] = total_ref[h * 72 : (h + 1) * 72].astype(BF)


def project(where, lines, basis, other_basis):
    cols, rows = basis.shape
    deep = rows
    line = pl.BlockSpec((VALID, deep), lambda k: (0, k))
    rotated = pl.BlockSpec((cols, deep), lambda k: (0, k))
    return pl.pallas_call(
        project_kernel,
        grid=(rows // deep,),
        in_specs=[pl.BlockSpec(memory_space=pltpu.SMEM)] + [line] * 4 + [rotated] * 2,
        out_specs=pl.BlockSpec((4, 72, cols), lambda k: (0, 0, 0)),
        out_shape=like(4, 72, cols),
        scratch_shapes=[pltpu.VMEM((2, 2, VALID, deep), BF), pltpu.VMEM((2 * VALID, cols), F32)],
        compiler_params=PARAMS,
        cost_estimate=LONG,
    )(where, *lines, basis, other_basis)


def sum_kernel(parts_ref, out_ref):
    total = parts_ref[0].astype(F32)
    for x in range(1, 4):
        total += parts_ref[x].astype(F32)
    out_ref[...] = total.astype(BF)


def spread_kernel(one_ref, two_ref, out_ref):
    total = (one_ref[...].astype(F32) + two_ref[...].astype(F32)).astype(BF)
    for x in range(4):
        out_ref[x] = total


def arrange_kernel(where_ref, own_ref, other_ref, out_ref, mask_ref):
    core = where_ref[3]
    slot = lax.broadcasted_iota(jnp.int32, (8, VALID), 1).astype(F32)
    for zhi in range(2):
        for c in range(2):
            mine = core == c
            g = zhi * 2 + c
            for y in range(4):
                k = y ^ where_ref[5]
                block = jnp.where(mine, own_ref[k, zhi], other_ref[k, zhi])
                out_ref[g, :, y * WIDE : (y + 1) * WIDE] = block[:VALID]
            count = block[VALID:, :VALID].astype(F32)
            mask_ref[g] = (slot < count).astype(F32).astype(BF)


def left_kernel(lines_ref, left_ref):
    for t in range(2):
        left_ref[t] = lines_ref[t].T


def square_kernel(where_ref, own_ref, other_ref, in_ref, mask_ref, eig_ref, left_ref):
    core = where_ref[3]

    @pl.when(pl.program_id(0) == 0)
    def _():
        for t in range(2):
            for at, lines in (
                (2 * core + t, own_ref[t]),
                (2 * (1 - core) + t, other_ref[t].T),
            ):
                first = lines * mask_ref[at][:1]
                left_ref[2 * at] = first
                left_ref[2 * at + 1] = lines - first

    rows = 112
    for o in range(448 // rows):
        total = jnp.zeros((rows, eig_ref.shape[1]), F32)
        for s in range(8):
            block = jnp.dot(
                left_ref[s, o * rows : (o + 1) * rows, :],
                in_ref[s // 2],
                preferred_element_type=F32,
            )
            total += block * block
        eig_ref[o * rows : (o + 1) * rows] = total / 768.0


def squares(where, left, other, ins, masks):
    cols, wide, tile = left.shape[1], ins.shape[2], ins.shape[2]
    whole = lambda x: pl.BlockSpec(x.shape, lambda i: (0, 0, 0))
    return pl.pallas_call(
        square_kernel,
        grid=(wide // tile,),
        in_specs=[
            pl.BlockSpec(memory_space=pltpu.SMEM),
            whole(left),
            whole(other),
            pl.BlockSpec((4, VALID, tile), lambda i: (0, 0, i)),
            whole(masks),
        ],
        out_specs=pl.BlockSpec((cols, tile), lambda i: (0, i)),
        out_shape=like(cols, wide, dtype=F32),
        scratch_shapes=[pltpu.VMEM((8, cols, VALID), BF)],
        compiler_params=PARAMS,
    )(where, left, other, ins, masks)


def call(kernel, out, *args, scalars=1, scratch=(), cost=None):
    single = not isinstance(out, (list, tuple))
    smem = pl.BlockSpec(memory_space=pltpu.SMEM)
    vmem = pl.BlockSpec(memory_space=pltpu.VMEM)
    outs = [out] if single else list(out)
    got = pl.pallas_call(
        kernel,
        in_specs=[smem] * scalars + [vmem] * (len(args) - scalars),
        out_specs=[vmem] * len(outs),
        out_shape=outs,
        scratch_shapes=scratch,
        cost_estimate=cost,
        compiler_params=PARAMS,
    )(*args)
    return got[0] if single else got


def like(*shape, dtype=BF):
    return jax.ShapeDtypeStruct(shape, dtype)


def others(x, axis):
    n = lax.axis_size(axis)
    sent = {k: lax.ppermute(x, axis, [(i, i ^ k) for i in range(n)]) for k in (1, 3, 2)}
    return [sent[k] for k in (1, 2, 3)]


def per_device(acts, grads, basis_in, basis_out, lengths):
    zhi, core, y, zh, zq = (lax.axis_index(a) for a in ("zhi", "core", "y", "zh", "zq"))
    crossed = (core != zhi).astype(jnp.int32)
    tokens = (y >> 1) ^ zhi
    where = jnp.stack([zh, crossed, lengths[0, 0], core, zq, y, (y & 1) ^ tokens, tokens])
    lines, partial = pl.pallas_call(
        start_kernel,
        in_specs=[pl.BlockSpec(memory_space=pltpu.SMEM)] + [pl.BlockSpec(memory_space=pl.ANY)] * 3,
        out_specs=[pl.BlockSpec(memory_space=pltpu.VMEM)] * 2,
        out_shape=[like(VALID, WIDE), like(4, VALID, WIDE)],
        scratch_shapes=[pltpu.VMEM(x.shape, BF) for x in (acts, basis_in, grads)]
        + [pltpu.SemaphoreType.DMA] * 3,
        compiler_params=pltpu.CompilerParams(vmem_limit_bytes=60 << 20),
    )(lengths, grads, acts, basis_in)
    near = lax.ppermute(lines, PLANE, to_basis(False))
    far = lax.ppermute(lines, PLANE, to_basis(True))
    partial = exchange(partial, "y")
    basis = basis_out[0].T
    cols = basis.shape[0]
    other_basis = swap(basis, "core")
    both = call(pair_kernel, like(2, VALID, WIDE), near, far, scalars=0, cost=HINT)
    both = call(join_kernel, like(4, 2, VALID, WIDE), both, partial, scalars=0)
    both = exchange(both, "zq")
    lines, ins = call(sort_kernel, [like(VALID, 8 * FEAT), like(16, 80, 128)], where, both)
    lines = [lines] + others(lines, "y")
    ins = exchange(ins, ("zhi", "zh", "zq"))
    part = project(where, lines, basis, other_basis)
    part, ins = lax.optimization_barrier((part, ins))
    ins = call(merge_kernel, like(2, VALID + 8, WIDE), ins, scalars=0)
    part = exchange(part, "x")
    part = call(sum_kernel, like(72, cols), part, scalars=0)
    part, ins = lax.optimization_barrier((part, ins))
    ins = [ins] + others(ins, "y")
    part = call(spread_kernel, like(4, 72, cols), part, swap(part, "zhi"), scalars=0, cost=HINT)
    ins = jnp.stack(ins)
    other_ins = swap(ins, "core")
    outs = exchange(part, "x").reshape(2, VALID, cols)
    ins, masks = call(
        arrange_kernel,
        [like(4, VALID, 1024), like(4, 8, VALID)],
        where,
        ins,
        other_ins,
    )
    left = call(left_kernel, like(2, cols, VALID), outs, scalars=0, cost=HINT)
    return squares(where, left, swap(outs, "core"), ins, masks)


def solution(mesh):
    axes = ("zhi", "core", "x", "y", "zh", "zq")
    fine = Mesh(mesh.devices.reshape(2, 2, 4, 4, 2, 4), axes)
    grp, row, col = ("zhi", "core"), "x", ("y", "zh", "zq")
    in_specs = (
        P(grp, col),
        P(grp, (row, *col)),
        P(col, row),
        P(row, grp, col),
        P(grp, None),
    )
    return jax.shard_map(
        per_device, mesh=fine, in_specs=in_specs, out_specs=P(col, row), check_vma=False
    )
```

```python
import jax
import jax.numpy as jnp
from jax import lax
from jax.experimental import pallas as pl
from jax.experimental.pallas import tpu as pltpu
from jax.sharding import Mesh, PartitionSpec as P

LEN = 96
VALID = 144
FEAT = 224
WIDE = 256
BF = jnp.bfloat16
F32 = jnp.float32
HINT = pl.CostEstimate(flops=int(5e9), bytes_accessed=int(1e6), transcendentals=0)
LONG = pl.CostEstimate(flops=int(3e10), bytes_accessed=int(1e6), transcendentals=0)
PLANE = ("zhi", "core", "y", "zh", "zq")
PARAMS = pltpu.CompilerParams(vmem_limit_bytes=16 << 20)


def to_basis(far):
    def place(zhi, core, y, zlo):
        return ((zhi * 2 + core) * 4 + y) * 8 + zlo

    pairs = []
    for zhi in range(2):
        for core in range(2):
            for y in range(4):
                for z in range(8):
                    crossed = zhi != y >> 1
                    to = (z ^ 3 if far else z ^ 4) if crossed else (z ^ 4 if far else z)
                    to_y = 2 * (core ^ (y >> 1)) + ((y & 1) ^ core)
                    there = place(y >> 1, zhi, to_y, to)
                    pairs.append((place(zhi, core, y, z), there))
    return pairs


def exchange(x, axis):
    return lax.all_to_all(x, axis, 0, 0, tiled=True)


def everywhere(x, axis):
    return exchange(jnp.broadcast_to(x[None], (lax.axis_size(axis),) + x.shape), axis)


def swap(x, axis):
    return lax.ppermute(x, axis, [(0, 1), (1, 0)])


def across(left, right):
    return lax.dot_general(left, right, (((1,), (1,)), ((), ())), preferred_element_type=F32)


def chosen(first):
    slot = lax.broadcasted_iota(jnp.int32, (VALID, 2 * LEN), 0)
    line = lax.broadcasted_iota(jnp.int32, (VALID, 2 * LEN), 1)
    source = jnp.where(slot < first, slot, slot - first + LEN)
    return (source == line).astype(F32).astype(BF)


def start_kernel(len_ref, grads_hbm, acts_hbm, basis_hbm, lines_ref, part_ref, *scratch):
    held, sems = scratch[:3], scratch[3:]
    copies = [
        pltpu.make_async_copy(source, ref, sem)
        for source, ref, sem in zip((acts_hbm, basis_hbm, grads_hbm), held, sems)
    ]
    for copy in copies:
        copy.start()
    acts_ref, basis_ref, grads_ref = held
    pick = chosen(len_ref[0, 0])
    copies[0].wait()
    lines = jnp.dot(pick, acts_ref[...], preferred_element_type=F32).astype(BF)
    copies[1].wait()
    for y in range(4):
        part_ref[y] = jnp.dot(
            lines, basis_ref[:, y * WIDE : (y + 1) * WIDE], preferred_element_type=F32
        ).astype(BF)
    copies[2].wait()
    lines_ref[:, :FEAT] = jnp.dot(pick, grads_ref[...], preferred_element_type=F32).astype(BF)
    lines_ref[:, FEAT:] = jnp.zeros((VALID, WIDE - FEAT), BF)


def pair_kernel(near_ref, far_ref, out_ref):
    out_ref[0] = near_ref[...]
    out_ref[1] = far_ref[...]


def join_kernel(pair_ref, parts_ref, out_ref):
    total = parts_ref[0].astype(F32)
    for y in range(1, 4):
        total += parts_ref[y].astype(F32)
    total = total.astype(BF)
    for d in range(4):
        for w in range(2):
            at = d * 64 + w * 32
            out_ref[d, w] = jnp.concatenate(
                [pair_ref[w][:, :FEAT], total[:, at : at + 32]], axis=1
            )


def sort_kernel(where_ref, both_ref, out_ref, in_ref):
    zh, crossed = where_ref[0], where_ref[1]
    for f in range(8):
        far = (jnp.int32(f // 4) != zh).astype(jnp.int32) ^ crossed
        at = (f % 4) ^ (3 * (far & crossed))
        out_ref[:, f * FEAT : (f + 1) * FEAT] = both_ref[at, far][:, :FEAT]
    sums = []
    for w in range(2):
        total = both_ref[0, w][:, FEAT:].astype(F32)
        for q in range(1, 4):
            total += both_ref[q, w][:, FEAT:].astype(F32)
        sums.append(total)
    half = VALID // 2
    packed = jnp.concatenate([x[i : i + half] for i in (0, half) for x in sums], axis=1)
    count = jnp.full((8, 128), where_ref[2], jnp.int32).astype(F32).astype(BF)
    for copy in range(16):
        in_ref[copy, :half] = packed.astype(BF)
        in_ref[copy, half:] = count


def merge_kernel(parts_ref, out_ref):
    half = VALID // 2
    for zhi in range(2):
        for q in range(4):
            at = zhi * 8 + q
            total = parts_ref[at, :half].astype(F32) + parts_ref[at + 4, :half].astype(F32)
            total = total.astype(BF)
            out_ref[zhi, :half, q * 64 : q * 64 + 64] = total[:, :64]
            out_ref[zhi, half:VALID, q * 64 : q * 64 + 64] = total[:, 64:]
        for h in range(2):
            out_ref[zhi, VALID:, h * 128 : h * 128 + 128] = parts_ref[zhi * 8, half:]


def project_kernel(
    where_ref, a_ref, b_ref, c_ref, d_ref, own_ref, other_ref, out_ref, held, total_ref
):
    step = pl.program_id(0)
    tokens, same = where_ref[7], where_ref[3] == where_ref[6]
    for left_ref, right_ref, t in ((a_ref, b_ref, tokens), (d_ref, c_ref, 1 - tokens)):
        left, right = left_ref[...], right_ref[...]
        held[0, t] = jnp.where(same, left, right)
        held[1, t] = jnp.where(same, right, left)
    rows = (2 * VALID, held.shape[3])
    total = across(held[0].reshape(rows), own_ref[...])
    total += across(held[1].reshape(rows), other_ref[...])

    @pl.when(step == 0)
    def _():
        total_ref[...] = total

    @pl.when(step > 0)
    def _():
        total_ref[...] += total

    @pl.when(step == pl.num_programs(0) - 1)
    def _():
        for h in range(4):
            out_ref[h] = total_ref[h * 72 : (h + 1) * 72].astype(BF)


def project(where, lines, basis, other_basis):
    cols, rows = basis.shape
    deep = rows
    line = pl.BlockSpec((VALID, deep), lambda k: (0, k))
    rotated = pl.BlockSpec((cols, deep), lambda k: (0, k))
    return pl.pallas_call(
        project_kernel,
        grid=(rows // deep,),
        in_specs=[pl.BlockSpec(memory_space=pltpu.SMEM)] + [line] * 4 + [rotated] * 2,
        out_specs=pl.BlockSpec((4, 72, cols), lambda k: (0, 0, 0)),
        out_shape=like(4, 72, cols),
        scratch_shapes=[pltpu.VMEM((2, 2, VALID, deep), BF), pltpu.VMEM((2 * VALID, cols), F32)],
        compiler_params=PARAMS,
        cost_estimate=LONG,
    )(where, *lines, basis, other_basis)


def sum_kernel(parts_ref, out_ref):
    total = parts_ref[0].astype(F32)
    for x in range(1, 4):
        total += parts_ref[x].astype(F32)
    out_ref[...] = total.astype(BF)


def spread_kernel(one_ref, two_ref, out_ref):
    total = (one_ref[...].astype(F32) + two_ref[...].astype(F32)).astype(BF)
    for x in range(4):
        out_ref[x] = total


def arrange_kernel(where_ref, own_ref, other_ref, out_ref, mask_ref):
    core = where_ref[3]
    slot = lax.broadcasted_iota(jnp.int32, (8, VALID), 1).astype(F32)
    for zhi in range(2):
        for c in range(2):
            mine = core == c
            g = zhi * 2 + c
            for y in range(4):
                k = y ^ where_ref[5]
                block = jnp.where(mine, own_ref[k, zhi], other_ref[k, zhi])
                out_ref[g, :, y * WIDE : (y + 1) * WIDE] = block[:VALID]
            count = block[VALID:, :VALID].astype(F32)
            mask_ref[g] = (slot < count).astype(F32).astype(BF)


def left_kernel(lines_ref, left_ref):
    for t in range(2):
        left_ref[t] = lines_ref[t].T


def square_kernel(own_ref, other_ref, in_ref, mask_ref, eig_ref, left_ref):
    core = lax.axis_index("core")

    @pl.when(pl.program_id(0) == 0)
    def _():
        for t in range(2):
            for at, lines in (
                (2 * core + t, own_ref[t]),
                (2 * (1 - core) + t, other_ref[t].T),
            ):
                first = lines * mask_ref[at][:1]
                left_ref[2 * at] = first
                left_ref[2 * at + 1] = lines - first

    rows = 112
    for o in range(448 // rows):
        total = jnp.zeros((rows, eig_ref.shape[1]), F32)
        for s in range(8):
            block = jnp.dot(
                left_ref[s, o * rows : (o + 1) * rows, :],
                in_ref[s // 2],
                preferred_element_type=F32,
            )
            total += block * block
        eig_ref[o * rows : (o + 1) * rows] = total * (1.0 / 768.0)


def squares(left, other, ins, masks):
    cols, wide, tile = left.shape[1], ins.shape[2], ins.shape[2]
    whole = lambda x: pl.BlockSpec(x.shape, lambda i: (0, 0, 0))
    return pl.pallas_call(
        square_kernel,
        grid=(wide // tile,),
        in_specs=[
            whole(left),
            whole(other),
            pl.BlockSpec((4, VALID, tile), lambda i: (0, 0, i)),
            whole(masks),
        ],
        out_specs=pl.BlockSpec((cols, tile), lambda i: (0, i)),
        out_shape=like(cols, wide, dtype=F32),
        scratch_shapes=[pltpu.VMEM((8, cols, VALID), BF)],
        compiler_params=PARAMS,
    )(left, other, ins, masks)


def call(kernel, out, *args, scalars=1, scratch=(), cost=None):
    single = not isinstance(out, (list, tuple))
    smem = pl.BlockSpec(memory_space=pltpu.SMEM)
    vmem = pl.BlockSpec(memory_space=pltpu.VMEM)
    outs = [out] if single else list(out)
    got = pl.pallas_call(
        kernel,
        in_specs=[smem] * scalars + [vmem] * (len(args) - scalars),
        out_specs=[vmem] * len(outs),
        out_shape=outs,
        scratch_shapes=scratch,
        cost_estimate=cost,
        compiler_params=PARAMS,
    )(*args)
    return got[0] if single else got


def like(*shape, dtype=BF):
    return jax.ShapeDtypeStruct(shape, dtype)


def others(x, axis):
    n = lax.axis_size(axis)
    sent = {k: lax.ppermute(x, axis, [(i, i ^ k) for i in range(n)]) for k in (1, 3, 2)}
    return [sent[k] for k in (1, 2, 3)]


def per_device(acts, grads, basis_in, basis_out, lengths):
    zhi, core, y, zh, zq = (lax.axis_index(a) for a in ("zhi", "core", "y", "zh", "zq"))
    crossed = (core != zhi).astype(jnp.int32)
    tokens = (y >> 1) ^ zhi
    where = jnp.stack([zh, crossed, lengths[0, 0], core, zq, y, (y & 1) ^ tokens, tokens])
    lines, partial = pl.pallas_call(
        start_kernel,
        in_specs=[pl.BlockSpec(memory_space=pltpu.SMEM)] + [pl.BlockSpec(memory_space=pl.ANY)] * 3,
        out_specs=[pl.BlockSpec(memory_space=pltpu.VMEM)] * 2,
        out_shape=[like(VALID, WIDE), like(4, VALID, WIDE)],
        scratch_shapes=[pltpu.VMEM(x.shape, BF) for x in (acts, basis_in, grads)]
        + [pltpu.SemaphoreType.DMA] * 3,
        compiler_params=pltpu.CompilerParams(vmem_limit_bytes=60 << 20),
    )(lengths, grads, acts, basis_in)
    near = lax.ppermute(lines, PLANE, to_basis(False))
    far = lax.ppermute(lines, PLANE, to_basis(True))
    partial = exchange(partial, "y")
    basis = basis_out[0].T
    cols = basis.shape[0]
    other_basis = swap(basis, "core")
    both = call(pair_kernel, like(2, VALID, WIDE), near, far, scalars=0, cost=HINT)
    both = call(join_kernel, like(4, 2, VALID, WIDE), both, partial, scalars=0)
    both = exchange(both, "zq")
    lines, ins = call(sort_kernel, [like(VALID, 8 * FEAT), like(16, 80, 128)], where, both)
    lines = [lines] + others(lines, "y")
    ins = exchange(ins, ("zhi", "zh", "zq"))
    part = project(where, lines, basis, other_basis)
    part, ins = lax.optimization_barrier((part, ins))
    ins = call(merge_kernel, like(2, VALID + 8, WIDE), ins, scalars=0)
    part = exchange(part, "x")
    part = call(sum_kernel, like(72, cols), part, scalars=0)
    part, ins = lax.optimization_barrier((part, ins))
    ins = [ins] + others(ins, "y")
    part = call(spread_kernel, like(4, 72, cols), part, swap(part, "zhi"), scalars=0, cost=HINT)
    ins = jnp.stack(ins)
    other_ins = swap(ins, "core")
    outs = exchange(part, "x").reshape(2, VALID, cols)
    ins, masks = call(
        arrange_kernel,
        [like(4, VALID, 1024), like(4, 8, VALID)],
        where,
        ins,
        other_ins,
    )
    left = call(left_kernel, like(2, cols, VALID), outs, scalars=0, cost=HINT)
    return squares(left, swap(outs, "core"), ins, masks)


def solution(mesh):
    axes = ("zhi", "core", "x", "y", "zh", "zq")
    fine = Mesh(mesh.devices.reshape(2, 2, 4, 4, 2, 4), axes)
    grp, row, col = ("zhi", "core"), "x", ("y", "zh", "zq")
    in_specs = (
        P(grp, col),
        P(grp, (row, *col)),
        P(col, row),
        P(row, grp, col),
        P(grp, None),
    )
    return jax.shard_map(
        per_device, mesh=fine, in_specs=in_specs, out_specs=P(col, row), check_vma=False
    )
```

```python
import jax
import jax.numpy as jnp
from jax import lax
from jax.experimental import pallas as pl
from jax.experimental.pallas import tpu as pltpu
from jax.sharding import Mesh, PartitionSpec as P

LEN = 96
VALID = 144
FEAT = 224
WIDE = 256
BF = jnp.bfloat16
F32 = jnp.float32
HINT = pl.CostEstimate(flops=int(5e9), bytes_accessed=int(1e6), transcendentals=0)
LONG = pl.CostEstimate(flops=int(3e10), bytes_accessed=int(1e6), transcendentals=0)
PLANE = ("zhi", "core", "y", "zh", "zq")
PARAMS = pltpu.CompilerParams(vmem_limit_bytes=16 << 20)


def to_basis(far):
    def place(zhi, core, y, zlo):
        return ((zhi * 2 + core) * 4 + y) * 8 + zlo

    pairs = []
    for zhi in range(2):
        for core in range(2):
            for y in range(4):
                for z in range(8):
                    crossed = zhi != y >> 1
                    to = (z ^ 3 if far else z ^ 4) if crossed else (z ^ 4 if far else z)
                    to_y = 2 * (core ^ (y >> 1)) + ((y & 1) ^ core)
                    there = place(y >> 1, zhi, to_y, to)
                    pairs.append((place(zhi, core, y, z), there))
    return pairs


def exchange(x, axis):
    return lax.all_to_all(x, axis, 0, 0, tiled=True)


def everywhere(x, axis):
    return exchange(jnp.broadcast_to(x[None], (lax.axis_size(axis),) + x.shape), axis)


def swap(x, axis):
    return lax.ppermute(x, axis, [(0, 1), (1, 0)])


def across(left, right):
    return lax.dot_general(left, right, (((1,), (1,)), ((), ())), preferred_element_type=F32)


def chosen(first):
    slot = lax.broadcasted_iota(jnp.int32, (VALID, 2 * LEN), 0)
    line = lax.broadcasted_iota(jnp.int32, (VALID, 2 * LEN), 1)
    source = jnp.where(slot < first, slot, slot - first + LEN)
    return (source == line).astype(F32).astype(BF)


def start_kernel(len_ref, grads_hbm, acts_hbm, basis_hbm, lines_ref, part_ref, *scratch):
    held, sems = scratch[:3], scratch[3:]
    copies = [
        pltpu.make_async_copy(source, ref, sem)
        for source, ref, sem in zip((acts_hbm, basis_hbm, grads_hbm), held, sems)
    ]
    for copy in copies:
        copy.start()
    acts_ref, basis_ref, grads_ref = held
    pick = chosen(len_ref[0, 0])
    copies[0].wait()
    lines = jnp.dot(pick, acts_ref[...], preferred_element_type=F32).astype(BF)
    copies[1].wait()
    for y in range(4):
        part_ref[y] = jnp.dot(
            lines, basis_ref[:, y * WIDE : (y + 1) * WIDE], preferred_element_type=F32
        ).astype(BF)
    copies[2].wait()
    lines_ref[:, :FEAT] = jnp.dot(pick, grads_ref[...], preferred_element_type=F32).astype(BF)
    lines_ref[:, FEAT:] = jnp.zeros((VALID, WIDE - FEAT), BF)


def pair_kernel(near_ref, far_ref, out_ref):
    out_ref[0] = near_ref[...]
    out_ref[1] = far_ref[...]


def join_kernel(pair_ref, parts_ref, out_ref):
    total = parts_ref[0].astype(F32)
    for y in range(1, 4):
        total += parts_ref[y].astype(F32)
    total = total.astype(BF)
    for d in range(4):
        for w in range(2):
            at = d * 64 + w * 32
            out_ref[d, w] = jnp.concatenate(
                [pair_ref[w][:, :FEAT], total[:, at : at + 32]], axis=1
            )


def sort_kernel(len_ref, both_ref, out_ref, in_ref):
    zh = lax.axis_index("zh")
    crossed = (lax.axis_index("core") != lax.axis_index("zhi")).astype(jnp.int32)
    for f in range(8):
        far = (jnp.int32(f // 4) != zh).astype(jnp.int32) ^ crossed
        at = (f % 4) ^ (3 * (far & crossed))
        out_ref[:, f * FEAT : (f + 1) * FEAT] = both_ref[at, far][:, :FEAT]
    sums = []
    for w in range(2):
        total = both_ref[0, w][:, FEAT:].astype(F32)
        for q in range(1, 4):
            total += both_ref[q, w][:, FEAT:].astype(F32)
        sums.append(total)
    half = VALID // 2
    packed = jnp.concatenate([x[i : i + half] for i in (0, half) for x in sums], axis=1)
    count = jnp.broadcast_to(len_ref[:, :1].astype(F32), (8, 128)).astype(BF)
    for copy in range(16):
        in_ref[copy, :half] = packed.astype(BF)
        in_ref[copy, half:] = count


def merge_kernel(parts_ref, out_ref):
    half = VALID // 2
    for zhi in range(2):
        for q in range(4):
            at = zhi * 8 + q
            total = parts_ref[at, :half].astype(F32) + parts_ref[at + 4, :half].astype(F32)
            total = total.astype(BF)
            out_ref[zhi, :half, q * 64 : q * 64 + 64] = total[:, :64]
            out_ref[zhi, half:VALID, q * 64 : q * 64 + 64] = total[:, 64:]
        for h in range(2):
            out_ref[zhi, VALID:, h * 128 : h * 128 + 128] = parts_ref[zhi * 8, half:]


def project_kernel(
    a_ref, b_ref, c_ref, d_ref, own_ref, other_ref, out_ref, held, total_ref
):
    step, y = pl.program_id(0), lax.axis_index("y")
    tokens = (y >> 1) ^ lax.axis_index("zhi")
    same = lax.axis_index("core") == (y & 1) ^ tokens
    for left_ref, right_ref, t in ((a_ref, b_ref, tokens), (d_ref, c_ref, 1 - tokens)):
        left, right = left_ref[...], right_ref[...]
        held[0, t] = jnp.where(same, left, right)
        held[1, t] = jnp.where(same, right, left)
    rows = (2 * VALID, held.shape[3])
    total = across(held[0].reshape(rows), own_ref[...])
    total += across(held[1].reshape(rows), other_ref[...])

    @pl.when(step == 0)
    def _():
        total_ref[...] = total

    @pl.when(step > 0)
    def _():
        total_ref[...] += total

    @pl.when(step == pl.num_programs(0) - 1)
    def _():
        for h in range(4):
            out_ref[h] = total_ref[h * 72 : (h + 1) * 72].astype(BF)


def project(lines, basis, other_basis):
    cols, rows = basis.shape
    deep = rows
    line = pl.BlockSpec((VALID, deep), lambda k: (0, k))
    rotated = pl.BlockSpec((cols, deep), lambda k: (0, k))
    return pl.pallas_call(
        project_kernel,
        grid=(rows // deep,),
        in_specs=[line] * 4 + [rotated] * 2,
        out_specs=pl.BlockSpec((4, 72, cols), lambda k: (0, 0, 0)),
        out_shape=like(4, 72, cols),
        scratch_shapes=[pltpu.VMEM((2, 2, VALID, deep), BF), pltpu.VMEM((2 * VALID, cols), F32)],
        compiler_params=PARAMS,
        cost_estimate=LONG,
    )(*lines, basis, other_basis)


def sum_kernel(parts_ref, out_ref):
    total = parts_ref[0].astype(F32)
    for x in range(1, 4):
        total += parts_ref[x].astype(F32)
    out_ref[...] = total.astype(BF)


def spread_kernel(one_ref, two_ref, out_ref):
    total = (one_ref[...].astype(F32) + two_ref[...].astype(F32)).astype(BF)
    for x in range(4):
        out_ref[x] = total


def arrange_kernel(own_ref, other_ref, out_ref, mask_ref):
    core, own_y = lax.axis_index("core"), lax.axis_index("y")
    slot = lax.broadcasted_iota(jnp.int32, (8, VALID), 1).astype(F32)
    for zhi in range(2):
        for c in range(2):
            mine = core == c
            g = zhi * 2 + c
            for y in range(4):
                k = y ^ own_y
                block = jnp.where(mine, own_ref[k, zhi], other_ref[k, zhi])
                out_ref[g, :, y * WIDE : (y + 1) * WIDE] = block[:VALID]
            count = block[VALID:, :VALID].astype(F32)
            mask_ref[g] = (slot < count).astype(F32).astype(BF)


def left_kernel(lines_ref, left_ref):
    for t in range(2):
        left_ref[t] = lines_ref[t].T


def square_kernel(own_ref, other_ref, in_ref, mask_ref, eig_ref, left_ref):
    core = lax.axis_index("core")

    @pl.when(pl.program_id(0) == 0)
    def _():
        for t in range(2):
            for at, lines in (
                (2 * core + t, own_ref[t]),
                (2 * (1 - core) + t, other_ref[t].T),
            ):
                first = lines * mask_ref[at][:1]
                left_ref[2 * at] = first
                left_ref[2 * at + 1] = lines - first

    rows = 112
    for o in range(448 // rows):
        total = jnp.zeros((rows, eig_ref.shape[1]), F32)
        for s in range(8):
            block = jnp.dot(
                left_ref[s, o * rows : (o + 1) * rows, :],
                in_ref[s // 2],
                preferred_element_type=F32,
            )
            total += block * block
        eig_ref[o * rows : (o + 1) * rows] = total * (1.0 / 768.0)


def squares(left, other, ins, masks):
    cols, wide, tile = left.shape[1], ins.shape[2], ins.shape[2]
    whole = lambda x: pl.BlockSpec(x.shape, lambda i: (0, 0, 0))
    return pl.pallas_call(
        square_kernel,
        grid=(wide // tile,),
        in_specs=[
            whole(left),
            whole(other),
            pl.BlockSpec((4, VALID, tile), lambda i: (0, 0, i)),
            whole(masks),
        ],
        out_specs=pl.BlockSpec((cols, tile), lambda i: (0, i)),
        out_shape=like(cols, wide, dtype=F32),
        scratch_shapes=[pltpu.VMEM((8, cols, VALID), BF)],
        compiler_params=PARAMS,
    )(left, other, ins, masks)


def call(kernel, out, *args, scalars=1, scratch=(), cost=None):
    single = not isinstance(out, (list, tuple))
    smem = pl.BlockSpec(memory_space=pltpu.SMEM)
    vmem = pl.BlockSpec(memory_space=pltpu.VMEM)
    outs = [out] if single else list(out)
    got = pl.pallas_call(
        kernel,
        in_specs=[smem] * scalars + [vmem] * (len(args) - scalars),
        out_specs=[vmem] * len(outs),
        out_shape=outs,
        scratch_shapes=scratch,
        cost_estimate=cost,
        compiler_params=PARAMS,
    )(*args)
    return got[0] if single else got


def like(*shape, dtype=BF):
    return jax.ShapeDtypeStruct(shape, dtype)


def others(x, axis):
    n = lax.axis_size(axis)
    sent = {k: lax.ppermute(x, axis, [(i, i ^ k) for i in range(n)]) for k in (1, 3, 2)}
    return [sent[k] for k in (1, 2, 3)]


def per_device(acts, grads, basis_in, basis_out, lengths):
    lines, partial = pl.pallas_call(
        start_kernel,
        in_specs=[pl.BlockSpec(memory_space=pltpu.SMEM)] + [pl.BlockSpec(memory_space=pl.ANY)] * 3,
        out_specs=[pl.BlockSpec(memory_space=pltpu.VMEM)] * 2,
        out_shape=[like(VALID, WIDE), like(4, VALID, WIDE)],
        scratch_shapes=[pltpu.VMEM(x.shape, BF) for x in (acts, basis_in, grads)]
        + [pltpu.SemaphoreType.DMA] * 3,
        compiler_params=pltpu.CompilerParams(vmem_limit_bytes=60 << 20),
    )(lengths, grads, acts, basis_in)
    near = lax.ppermute(lines, PLANE, to_basis(False))
    far = lax.ppermute(lines, PLANE, to_basis(True))
    partial = exchange(partial, "y")
    basis = basis_out[0].T
    cols = basis.shape[0]
    other_basis = swap(basis, "core")
    both = call(pair_kernel, like(2, VALID, WIDE), near, far, scalars=0, cost=HINT)
    both = call(join_kernel, like(4, 2, VALID, WIDE), both, partial, scalars=0)
    both = exchange(both, "zq")
    lines, ins = call(sort_kernel, [like(VALID, 8 * FEAT), like(16, 80, 128)], lengths, both, scalars=0)
    lines = [lines] + others(lines, "y")
    ins = exchange(ins, ("zhi", "zh", "zq"))
    part = project(lines, basis, other_basis)
    part, ins = lax.optimization_barrier((part, ins))
    ins = call(merge_kernel, like(2, VALID + 8, WIDE), ins, scalars=0)
    part = exchange(part, "x")
    part = call(sum_kernel, like(72, cols), part, scalars=0)
    part, ins = lax.optimization_barrier((part, ins))
    ins = [ins] + others(ins, "y")
    part = call(spread_kernel, like(4, 72, cols), part, swap(part, "zhi"), scalars=0, cost=HINT)
    ins = jnp.stack(ins)
    other_ins = swap(ins, "core")
    outs = exchange(part, "x").reshape(2, VALID, cols)
    ins, masks = call(
        arrange_kernel,
        [like(4, VALID, 1024), like(4, 8, VALID)],
        ins,
        other_ins,
        scalars=0,
    )
    left = call(left_kernel, like(2, cols, VALID), outs, scalars=0, cost=HINT)
    return squares(left, swap(outs, "core"), ins, masks)


def solution(mesh):
    axes = ("zhi", "core", "x", "y", "zh", "zq")
    fine = Mesh(mesh.devices.reshape(2, 2, 4, 4, 2, 4), axes)
    grp, row, col = ("zhi", "core"), "x", ("y", "zh", "zq")
    in_specs = (
        P(grp, col),
        P(grp, (row, *col)),
        P(col, row),
        P(row, grp, col),
        P(grp, None),
    )
    return jax.shard_map(
        per_device, mesh=fine, in_specs=in_specs, out_specs=P(col, row), check_vma=False
    )
```
